128 devices in a mesh: row: 8 (over y_lo, x), col: 16 (over z, y_hi, core).
Axes of the slice: x: 4, y: 4 (y_hi: 2, y_lo: 2; y = y_hi * 2 + y_lo), z: 4, core: 2. Of those that a mesh axis runs over, the one named last changes fastest.
Arguments:
- b_gate_up: bfloat16 [512, 28672], P('col', 'row'), may hold values from -6 to 6
- b_down: bfloat16 [256, 28672], P('col', 'row'), may hold values from -6 to 6
- a_gate_up: bfloat16 [512, 28672], P(None, 'row'), may hold values from -6 to 6
- a_down: bfloat16 [256, 28672], P(None, 'row'), may hold values from -6 to 6
- transform: bfloat16 [28672, 28672], P('row', 'col'), may hold values from -0.03125 to 0.03125
- check_tokens: bfloat16 [16384, 256], P('col'), may hold values from -6 to 6
Outputs:
- merged_gate_up: bfloat16 [512, 28672], P(None, 'row')
- merged_down: bfloat16 [256, 28672], P(None, 'row')
- check: bfloat16 [16384, 256], P('col', 'row')
The draws below stay inside these ranges and needn't reach their ends.
All inputs are finite; a program needn't handle non-finite values.
Results may differ from the reference program's by a relative error of at most 0.0081.
Values may be sent and summed in bfloat16 or wider, within the bound.
A program may use at most 128 MiB of HBM per device.

```python
import jax
import jax.numpy as jnp
from jax import lax

FF = 28672
R = 256
TOK_DEV = 1024
TOKENS = 16384
N_COL = 16


def level_of(own_key, dims, cuts, least, top_value):
    def one(axis_at, shards_of):
        steps = jax.random.uniform(jax.random.fold_in(jax.random.fold_in(own_key, 6), axis_at), (shards_of,), jnp.float32, least / len(cuts), top_value / len(cuts))
        return jnp.repeat(jnp.exp(steps), dims[axis_at] // shards_of).reshape((-1,) + (1,) * (len(dims) - axis_at - 1))

    factor_of = one(*cuts[0])
    for cut in cuts[1:]:
        factor_of = factor_of * one(*cut)
    return factor_of


def centred(stream_key, extent, width, reach, shards=(), dtype=jnp.bfloat16):
    drawn = jax.random.normal(stream_key, extent, jnp.float32) * width
    if len(shards) > 0:
        drawn = level_of(stream_key, extent, shards, -0.22, 0.18) * drawn
    return jnp.clip(drawn, min=-reach, max=reach).astype(dtype)


def setup_inputs(seed: int = 0) -> dict:
    key_of = jax.random.split(jax.random.key(seed), 7)
    b_gate_up = centred(key_of[0], (2 * R, FF), 1.0, 6.0, ((0, 16), (1, 8)))
    b_down = centred(key_of[1], (R, FF), 1.0, 6.0, ((0, 16), (1, 8)))
    a_gate_up = centred(key_of[2], (2 * R, FF), 1.0, 6.0, ((1, 8),))
    a_down = centred(key_of[3], (R, FF), 1.0, 6.0, ((1, 8),))
    transform = centred(key_of[4], (FF, FF), FF ** -0.5, 0.03125, ((0, 8), (1, 16)))
    check_tokens = centred(key_of[5], (TOKENS, R), 1.0, 6.0, ((0, 16),))
    return {"b_gate_up": b_gate_up, "b_down": b_down, "a_gate_up": a_gate_up, "a_down": a_down, "transform": transform, "check_tokens": check_tokens}


def reference(b_gate_up, b_down, a_gate_up, a_down, transform, check_tokens):
    projected_gate_up = jnp.dot(b_gate_up, transform, preferred_element_type=jnp.float32).astype(jnp.bfloat16)
    projected_down = jnp.dot(b_down, transform, preferred_element_type=jnp.float32).astype(jnp.bfloat16)
    merged_gate_up = (0.5 * (a_gate_up.astype(jnp.float32) + projected_gate_up.astype(jnp.float32))).astype(jnp.bfloat16)
    merged_down = (0.5 * (a_down.astype(jnp.float32) + projected_down.astype(jnp.float32))).astype(jnp.bfloat16)
    gate_weight = merged_gate_up[:R]
    up_weight = merged_gate_up[R:]

    def forward(block):
        gate = jnp.dot(block, gate_weight, preferred_element_type=jnp.float32) * (R ** -0.5)
        up = jnp.dot(block, up_weight, preferred_element_type=jnp.float32) * (R ** -0.5)
        hidden = (jax.nn.silu(gate) * up).astype(jnp.bfloat16)
        total = lax.dot_general(hidden, merged_down, (((1,), (1,)), ((), ())), preferred_element_type=jnp.float32)
        return (total * (FF ** -0.5)).astype(jnp.bfloat16)

    blocks = check_tokens.reshape(N_COL, TOK_DEV, R)
    check = lax.map(forward, blocks).reshape(TOKENS, R)
    return merged_gate_up, merged_down, check
```

```python
import jax
import jax.numpy as jnp
from jax import lax
from jax.experimental import pallas as pl
from jax.experimental.pallas import tpu as pltpu
from jax.sharding import PartitionSpec as P

FF = 28672
R = 256
MESH = pl.DeviceIdType.MESH
BF16 = jnp.bfloat16
F32 = jnp.float32
CHUNK, BLOCK, PIECE = 256, 16, 32
OFFSETS = ((2, 1), (2, 0), (1, 1), (3, 1), (1, 0), (3, 0), (0, 1))
HALF = 512


def device(x, y, z, core):
    x, y, z = lax.rem(x + 4, 4), lax.rem(y + 4, 4), lax.rem(z + 4, 4)
    return {"row": lax.rem(y, 2) * 4 + x, "col": z * 4 + (y // 2) * 2 + core}


def kernel(
    b_gate_up, b_down, a_gate_up, a_down, transform, tokens,
    out_gate_up, out_down, out_check,
    t_buf, b_buf, part, got, summed, moved, a_buf, merged, tok, tok_t, hidden, total, sent, got_check,
    local_sem, ag_send, ag_recv, rs_send, rs_recv, mv_send, mv_recv, ck_send, ck_recv,
):
    row, col = lax.axis_index("row"), lax.axis_index("col")
    x, y_lo = lax.rem(row, 4), row // 4
    z, y_hi, core = col // 4, lax.rem(col // 2, 2), lax.rem(col, 2)
    y = y_hi * 2 + y_lo
    other_core = 1 - core
    group = col // 2
    width = t_buf.shape[1]
    started = []

    def pair(z_off, flip):
        return lax.rem(z + z_off + 4, 4) * 2 + (1 - y_hi if flip else y_hi)

    def b_ref(i, g, k):
        return b_buf.at[i, pl.ds(pl.multiple_of((g * 2 + k) * BLOCK, BLOCK), BLOCK), :]

    def piece_of(g):
        return g + 1 - 2 * lax.rem(g, 2)

    def m_ref(i, g, k):
        rows = pl.ds(pl.multiple_of(piece_of(g) * PIECE, PIECE), PIECE)
        return merged.at[i, rows, pl.ds(pl.multiple_of(k * width, 128), width)]

    def p_rows(s):
        return pl.ds(pl.multiple_of(s * PIECE, PIECE), PIECE)

    up, down, far = device(x, y, z + 1, core), device(x, y, z - 1, core), device(x, y, z + 2, core)
    across, partner = device(x, y + 2, z, core), device(x, y, z, other_core)

    def by_row(dx, dy):
        return lax.rem(x + dx, 4) + 4 * lax.rem(y_lo + dy, 2)

    mv_to = {"row": group, "col": piece_of(row) * 2 + core}
    mv_from = {"row": piece_of(group), "col": row * 2 + core}

    t_copy = pltpu.make_async_copy(transform, t_buf, local_sem.at[0])
    own = []
    for i in range(3):
        src = b_gate_up.at[pl.ds(i * BLOCK, BLOCK), :] if i < 2 else b_down
        own.append(pltpu.make_async_copy(src, b_ref(i, group, core), local_sem.at[1 + i]))
        own[i].start()
    t_copy.start()
    tok_copy = pltpu.make_async_copy(tokens, tok, local_sem.at[4])
    tok_copy.start()
    mine = piece_of(group)
    a_copies = []
    for i in range(3):
        pairs, cols = pl.ds(mine * 2, 2), pl.ds(pl.multiple_of(core * width, 128), width)
        src = a_gate_up.at[pairs, i, :, cols] if i < 2 else a_down.at[pairs, :, cols]
        a_copies.append(pltpu.make_async_copy(src, a_buf.at[i], local_sem.at[5 + i]))
        a_copies[i].start()

    barrier = pltpu.get_barrier_semaphore()
    peers = [up, down, far, across, partner, mv_to, mv_from]
    peers += [{"row": by_row(dx, dy), "col": col} for dx, dy in OFFSETS]
    for peer in peers:
        pl.semaphore_signal(barrier, inc=1, device_id=peer, device_id_type=MESH)
    for i in range(3):
        own[i].wait()
    pl.semaphore_wait(barrier, len(peers))

    def send(src, dst, send_sem, recv_sem, to):
        copy = pltpu.make_async_remote_copy(
            src_ref=src, dst_ref=dst, send_sem=send_sem, recv_sem=recv_sem, device_id=to, device_id_type=MESH
        )
        copy.start()
        started.append(copy)

    def arrived(dst, send_sem, recv_sem, source):
        pltpu.make_async_remote_copy(
            src_ref=dst, dst_ref=dst, send_sem=send_sem, recv_sem=recv_sem, device_id=source, device_id_type=MESH
        ).wait_recv()

    def ag_pass(phase, ref, i, q, g, to):
        block = ref(i, g, core)
        send(block, block, ag_send.at[phase, i, q], ag_recv.at[phase, i, q], to)

    def ag_wait(phase, ref, i, q, g, k, source):
        arrived(ref(i, g, k), ag_send.at[phase, i, q], ag_recv.at[phase, i, q], source)

    def ag1(phase, ref, i):
        g = pair(0, False)
        for q, to in ((2, far), (3, across), (0, up), (1, down), (4, partner)):
            ag_pass(phase, ref, i, q, g, to)

    def ag2(phase, ref, i):
        g = pair(0, True)
        ag_wait(phase, ref, i, 3, g, core, across)
        ag_pass(phase, ref, i, 5, g, up)
        ag_pass(phase, ref, i, 6, g, down)
        g2 = pair(2, False)
        ag_wait(phase, ref, i, 2, g2, core, far)
        ag_pass(phase, ref, i, 7, g2, across)
        ag_pass(phase, ref, i, 8, g, partner)
        ag_pass(phase, ref, i, 9, g2, partner)
        for q, off, source in ((0, -1, down), (1, 1, up)):
            ag_wait(phase, ref, i, q, pair(off, False), core, source)
            ag_pass(phase, ref, i, 10 + q, pair(off, False), partner)

    def ag3(phase, ref, i):
        for q, off, source in ((5, -1, down), (6, 1, up), (7, 2, across)):
            ag_wait(phase, ref, i, q, pair(off, True), core, source)
            ag_pass(phase, ref, i, q + 7, pair(off, True), partner)
        for q, off, flip in (
            (4, 0, False), (8, 0, True), (9, 2, False), (10, -1, False), (11, 1, False),
            (12, -1, True), (13, 1, True), (14, 2, True),
        ):
            ag_wait(phase, ref, i, q, pair(off, flip), other_core, partner)

    def matmul(i, first, last):
        @pl.loop(first, last)
        def _(n):
            cols = pl.ds(pl.multiple_of(n * 256, 256), 256)
            part[i, :, cols] = jnp.dot(b_buf[i], t_buf[:, cols], preferred_element_type=F32).astype(BF16)

    def rs1(i):
        for q, (dx, dy) in enumerate(OFFSETS):
            s = by_row(dx, dy)
            send(part.at[i, p_rows(s), :], got.at[i, q], rs_send.at[i, q], rs_recv.at[i, q], {"row": s, "col": col})

    def rs2(i):
        for q, (dx, dy) in enumerate(OFFSETS):
            source = {"row": by_row(4 - dx, dy), "col": col}
            arrived(got.at[i, q], rs_send.at[i, q], rs_recv.at[i, q], source)

        @pl.loop(0, width // 256)
        def _(n):
            cols = pl.ds(pl.multiple_of(n * 256, 256), 256)
            value = part[i, p_rows(row), cols].astype(F32)
            for q in range(len(OFFSETS)):
                value = value + got[i, q, :, cols].astype(F32)
            summed[i, :, cols] = value.astype(BF16)

        send(summed.at[i], moved.at[i], mv_send.at[i], mv_recv.at[i], mv_to)

    def merge(i):
        a_copies[i].wait()
        arrived(moved.at[i], mv_send.at[i], mv_recv.at[i], mv_from)

        @pl.loop(0, width // 256)
        def _(n):
            cols = pl.ds(pl.multiple_of(n * 256, 256), 256)
            dst = pl.ds(pl.multiple_of(core * width + n * 256, 128), 256)
            a_part = a_buf[i, :, :, cols].reshape(PIECE, 256).astype(F32)
            value = 0.5 * (a_part + moved[i, :, cols].astype(F32))
            merged[i, p_rows(mine), dst] = value.astype(BF16)

        ag1(1, m_ref, i)

    out_copies = []

    def write_out(i):
        if i < 2:
            for c in range(16):
                copy = pltpu.make_async_copy(
                    merged.at[i, pl.ds(c * BLOCK, BLOCK), :], out_gate_up.at[c, i], local_sem.at[8 + i * 16 + c]
                )
                copy.start()
                out_copies.append(copy)
        else:
            copy = pltpu.make_async_copy(merged.at[2], out_down, local_sem.at[40])
            copy.start()
            out_copies.append(copy)

    def gate_up(first, last):
        @pl.loop(first, last)
        def _(n):
            cols = pl.ds(pl.multiple_of(n * 256, 256), 256)
            contract = (((0,), (0,)), ((), ()))
            weights = jnp.concatenate([merged[0, 0:128, cols], merged[1, 0:128, cols]], axis=0)
            gate = lax.dot_general(weights, tok_t[...], contract, preferred_element_type=F32) * R ** (-0.5)
            weights = jnp.concatenate([merged[0, 128:256, cols], merged[1, 128:256, cols]], axis=0)
            value = lax.dot_general(weights, tok_t[...], contract, preferred_element_type=F32) * R ** (-0.5)
            hidden[cols, :] = (gate * (0.5 + 0.5 * jnp.tanh(0.5 * gate)) * value).astype(BF16)

    def down_half(h):
        toks = pl.ds(h * HALF, HALF)
        value = jnp.dot(merged[2], hidden[:, toks], preferred_element_type=F32)
        total[h] = value
        sent[h] = value.astype(BF16)
        for q, (dx, dy) in enumerate(OFFSETS):
            s = by_row(dx, dy)
            send(sent.at[h, p_rows(s), :], got_check.at[h, q], ck_send.at[h, q], ck_recv.at[h, q], {"row": s, "col": col})

    def finish(h):
        for q, (dx, dy) in enumerate(OFFSETS):
            source = {"row": by_row(4 - dx, dy), "col": col}
            arrived(got_check.at[h, q], ck_send.at[h, q], ck_recv.at[h, q], source)
        value = total[h, p_rows(row), :]
        for q in range(len(OFFSETS)):
            value = value + got_check[h, q].astype(F32)
        out_check[:, h * HALF:(h + 1) * HALF] = (value * FF ** (-0.5)).astype(BF16)

    ag1(0, b_ref, 0)
    tok_copy.wait()
    turned = tok[...].T
    for c in range(8):
        for i in range(2):
            tok_t[i * 128 + c * 16:i * 128 + c * 16 + 16, :] = turned[c * 32 + i * 16:c * 32 + i * 16 + 16, :]
    ag2(0, b_ref, 0)
    ag1(0, b_ref, 1)
    ag3(0, b_ref, 0)
    t_copy.wait()
    matmul(0, 0, 4)
    ag2(0, b_ref, 1)
    ag1(0, b_ref, 2)
    matmul(0, 4, 7)
    rs1(0)
    ag3(0, b_ref, 1)
    matmul(1, 0, 4)
    ag2(0, b_ref, 2)
    matmul(1, 4, 7)
    rs1(1)
    ag3(0, b_ref, 2)
    matmul(2, 0, 4)
    rs2(0)
    matmul(2, 4, 7)
    rs1(2)
    merge(0)
    rs2(1)
    ag2(1, m_ref, 0)
    merge(1)
    ag3(1, m_ref, 0)
    write_out(0)
    rs2(2)
    ag2(1, m_ref, 1)
    merge(2)
    ag3(1, m_ref, 1)
    write_out(1)
    gate_up(0, 5)
    ag2(1, m_ref, 2)
    gate_up(5, 14)
    ag3(1, m_ref, 2)
    write_out(2)
    down_half(0)
    down_half(1)
    finish(0)
    finish(1)
    for copy in out_copies:
        copy.wait()
    for copy in started:
        copy.wait_send()


def on_device(b_gate_up, b_down, a_gate_up, a_down, transform, check_tokens):
    depth, width = transform.shape
    toks = check_tokens.shape[0]
    anywhere = pl.BlockSpec(memory_space=pl.ANY)
    merged_gate_up, merged_down, check = pl.pallas_call(
        kernel,
        out_shape=(
            jax.ShapeDtypeStruct((16, 2, BLOCK, depth), BF16),
            jax.ShapeDtypeStruct((CHUNK, depth), BF16),
            jax.ShapeDtypeStruct((PIECE, toks), BF16),
        ),
        in_specs=[anywhere] * 6,
        out_specs=(anywhere, anywhere, pl.BlockSpec(memory_space=pltpu.VMEM)),
        scratch_shapes=[
            pltpu.VMEM((depth, width), BF16),
            pltpu.VMEM((3, CHUNK, depth), BF16),
            pltpu.VMEM((3, CHUNK, width), BF16),
            pltpu.VMEM((3, 7, PIECE, width), BF16),
            pltpu.VMEM((3, PIECE, width), BF16),
            pltpu.VMEM((3, PIECE, width), BF16),
            pltpu.VMEM((3, 2, BLOCK, width), BF16),
            pltpu.VMEM((3, CHUNK, depth), BF16),
            pltpu.VMEM((toks, R), BF16),
            pltpu.VMEM((R, toks), BF16),
            pltpu.VMEM((depth, toks), BF16),
            pltpu.VMEM((2, CHUNK, HALF), F32),
            pltpu.VMEM((2, CHUNK, HALF), BF16),
            pltpu.VMEM((2, 7, PIECE, HALF), BF16),
            pltpu.SemaphoreType.DMA((41,)),
            pltpu.SemaphoreType.DMA((2, 3, 15)),
            pltpu.SemaphoreType.DMA((2, 3, 15)),
            pltpu.SemaphoreType.DMA((3, 7)),
            pltpu.SemaphoreType.DMA((3, 7)),
            pltpu.SemaphoreType.DMA((3,)),
            pltpu.SemaphoreType.DMA((3,)),
            pltpu.SemaphoreType.DMA((2, 7)),
            pltpu.SemaphoreType.DMA((2, 7)),
        ],
        compiler_params=pltpu.CompilerParams(
            collective_id=0, has_side_effects=True, vmem_limit_bytes=60 * 1024 * 1024
        ),
        name="merge_and_check",
    )(
        b_gate_up,
        b_down,
        a_gate_up.reshape(16, 2, BLOCK, depth),
        a_down.reshape(16, BLOCK, depth),
        transform,
        check_tokens,
    )
    return merged_gate_up.reshape(2 * R, depth), merged_down, check.T


def solution(mesh):
    return jax.shard_map(
        on_device,
        mesh=mesh,
        in_specs=(
            P("col", "row"),
            P("col", "row"),
            P(None, "row"),
            P(None, "row"),
            P("row", "col"),
            P("col", None),
        ),
        out_specs=(P(None, "row"), P(None, "row"), P("col", "row")),
        check_vma=False,
    )
```

```python
import jax
import jax.numpy as jnp
from jax import lax
from jax.experimental import pallas as pl
from jax.experimental.pallas import tpu as pltpu
from jax.sharding import PartitionSpec as P

FF = 28672
R = 256
MESH = pl.DeviceIdType.MESH
BF16 = jnp.bfloat16
F32 = jnp.float32
CHUNK, BLOCK, PIECE = 256, 16, 32
OFFSETS = ((2, 1), (2, 0), (1, 1), (3, 1), (1, 0), (3, 0), (0, 1))
HALF = 512


def device(x, y, z, core):
    x, y, z = lax.rem(x + 8, 4), lax.rem(y + 8, 4), lax.rem(z + 8, 4)
    return {"row": lax.rem(y, 2) * 4 + x, "col": z * 4 + (y // 2) * 2 + core}


def kernel(
    b_gate_up, b_down, a_gate_up, a_down, transform, tokens,
    out_gate_up, out_down, out_check,
    t_buf, b_buf, part, got, joined, kept, summed, passing, moved, a_buf, merged, tok, tok_t, hidden, total, sent, got_check,
    local_sem, ag_send, ag_recv, rs_send, rs_recv, mv_send, mv_recv, ck_send, ck_recv,
):
    row, col = lax.axis_index("row"), lax.axis_index("col")
    x, y_lo = lax.rem(row, 4), row // 4
    z, y_hi, core = col // 4, lax.rem(col // 2, 2), lax.rem(col, 2)
    y = y_hi * 2 + y_lo
    other_core = 1 - core
    group = col // 2
    width = t_buf.shape[1]
    started, moves = [], []

    def pair(z_off, flip):
        return lax.rem(z + z_off + 4, 4) * 2 + (1 - y_hi if flip else y_hi)

    def b_ref(i, g, k):
        return b_buf.at[i, pl.ds(pl.multiple_of((g * 2 + k) * BLOCK, BLOCK), BLOCK), :]

    from_z, from_y = row // 2, lax.rem(row, 2)

    def piece_of(g):
        return 2 * lax.rem(g // 2 - from_z + x + 6, 4) + lax.rem(g + from_y + y_lo, 2)

    def m_ref(i, g, k):
        rows = pl.ds(pl.multiple_of(piece_of(g) * PIECE, PIECE), PIECE)
        return merged.at[i, rows, pl.ds(pl.multiple_of(k * width, 128), width)]

    def p_rows(s):
        return pl.ds(pl.multiple_of(s * PIECE, PIECE), PIECE)

    up, down, far = device(x, y, z + 1, core), device(x, y, z - 1, core), device(x, y, z + 2, core)
    across, partner = device(x, y + 2, z, core), device(x, y, z, other_core)

    def by_row(dx, dy):
        return lax.rem(x + dx, 4) + 4 * lax.rem(y_lo + dy, 2)

    hop_z = lax.rem(z + x - 2 * lax.rem(z, 2) - y_hi + 7 + 3, 4)
    stays_z = hop_z == z
    lag = lax.rem(z - x + y_hi + 4, 4)
    src_z = lax.rem(lag + 2 * (1 - lax.rem(lag, 2)), 4)
    to_x, to_y_lo = 2 * lax.rem(src_z, 2) + y_hi, src_z // 2
    to_y_hi = lax.rem(y_hi + y_lo + to_y_lo, 2)
    stays_xy = (to_x == x) & (to_y_lo == y_lo) & (to_y_hi == y_hi)
    z_to, z_from = device(x, y, hop_z, core), device(x, y, src_z, core)
    xy_to = device(to_x, to_y_hi * 2 + to_y_lo, z, core)
    xy_from = device(z - from_z + x + 2, from_y * 2 + lax.rem(y_hi + from_y + y_lo, 2), z, core)
    ahead, behind, beside = device(x + 1, y, z, core), device(x - 1, y, z, core), device(x, y + 1 - 2 * y_lo, z, core)

    t_copy = pltpu.make_async_copy(transform, t_buf, local_sem.at[0])
    own = []
    for i in range(3):
        src = b_gate_up.at[pl.ds(i * BLOCK, BLOCK), :] if i < 2 else b_down
        own.append(pltpu.make_async_copy(src, b_ref(i, group, core), local_sem.at[1 + i]))
        own[i].start()
    t_copy.start()
    tok_copy = pltpu.make_async_copy(tokens, tok, local_sem.at[4])
    tok_copy.start()
    mine = piece_of(group)
    a_copies = []
    for i in range(3):
        pairs, cols = pl.ds(mine * 2, 2), pl.ds(pl.multiple_of(core * width, 128), width)
        src = a_gate_up.at[pairs, i, :, cols] if i < 2 else a_down.at[pairs, :, cols]
        a_copies.append(pltpu.make_async_copy(src, a_buf.at[i], local_sem.at[5 + i]))
        a_copies[i].start()

    barrier = pltpu.get_barrier_semaphore()
    peers = [up, down, far, across, partner, ahead, behind, beside, z_to, z_from, xy_to, xy_from]
    peers += [{"row": by_row(dx, dy), "col": col} for dx, dy in OFFSETS]
    for peer in peers:
        pl.semaphore_signal(barrier, inc=1, device_id=peer, device_id_type=MESH)
    for i in range(3):
        own[i].wait()
    pl.semaphore_wait(barrier, len(peers))

    def send(src, dst, send_sem, recv_sem, to):
        copy = pltpu.make_async_remote_copy(
            src_ref=src, dst_ref=dst, send_sem=send_sem, recv_sem=recv_sem, device_id=to, device_id_type=MESH
        )
        copy.start()
        started.append(copy)

    def arrived(dst, send_sem, recv_sem, source):
        pltpu.make_async_remote_copy(
            src_ref=dst, dst_ref=dst, send_sem=send_sem, recv_sem=recv_sem, device_id=source, device_id_type=MESH
        ).wait_recv()

    def ag_pass(phase, ref, i, q, g, to):
        block = ref(i, g, core)
        send(block, block, ag_send.at[phase, i, q], ag_recv.at[phase, i, q], to)

    def ag_wait(phase, ref, i, q, g, k, source):
        arrived(ref(i, g, k), ag_send.at[phase, i, q], ag_recv.at[phase, i, q], source)

    def ag1(phase, ref, i):
        g = pair(0, False)
        for q, to in ((2, far), (3, across), (0, up), (1, down), (4, partner)):
            ag_pass(phase, ref, i, q, g, to)

    def ag2(phase, ref, i):
        g = pair(0, True)
        ag_wait(phase, ref, i, 3, g, core, across)
        ag_pass(phase, ref, i, 5, g, up)
        ag_pass(phase, ref, i, 6, g, down)
        g2 = pair(2, False)
        ag_wait(phase, ref, i, 2, g2, core, far)
        ag_pass(phase, ref, i, 7, g2, across)
        ag_pass(phase, ref, i, 8, g, partner)
        ag_pass(phase, ref, i, 9, g2, partner)
        for q, off, source in ((0, -1, down), (1, 1, up)):
            ag_wait(phase, ref, i, q, pair(off, False), core, source)
            ag_pass(phase, ref, i, 10 + q, pair(off, False), partner)

    def ag3(phase, ref, i):
        for q, off, source in ((5, -1, down), (6, 1, up), (7, 2, across)):
            ag_wait(phase, ref, i, q, pair(off, True), core, source)
            ag_pass(phase, ref, i, q + 7, pair(off, True), partner)
        for q, off, flip in (
            (4, 0, False), (8, 0, True), (9, 2, False), (10, -1, False), (11, 1, False),
            (12, -1, True), (13, 1, True), (14, 2, True),
        ):
            ag_wait(phase, ref, i, q, pair(off, flip), other_core, partner)

    def matmul(i, first, last):
        @pl.loop(first, last)
        def _(n):
            cols = pl.ds(pl.multiple_of(n * 256, 256), 256)
            part[i, :, cols] = jnp.dot(b_buf[i], t_buf[:, cols], preferred_element_type=F32).astype(BF16)

    def part_piece(i, s):
        return part.at[i, p_rows(lax.rem(s + 8, 8)), :]

    def rs_pass(i, q, src, to):
        send(src, got.at[i, q], rs_send.at[i, q], rs_recv.at[i, q], to)

    def rs_wait(i, q, source):
        arrived(got.at[i, q], rs_send.at[i, q], rs_recv.at[i, q], source)

    def over_columns(body):
        @pl.loop(0, width // 256)
        def _(n):
            body(pl.ds(pl.multiple_of(n * 256, 256), 256))

    def rs1(i):
        rs_pass(i, 0, part_piece(i, 2 * x + 4), ahead)
        rs_pass(i, 1, part_piece(i, 2 * x + 5), behind)
        rs_pass(i, 2, part_piece(i, 2 * x + 3), ahead)
        rs_pass(i, 3, part_piece(i, 2 * x - 2), behind)

    def rs2(i):
        for q, s, to, source in ((0, 2 * x + 2, ahead, behind), (1, 2 * x - 1, behind, ahead)):
            rs_wait(i, q, source)
            rows = p_rows(lax.rem(s + 8, 8))

            def add(cols, q=q, rows=rows):
                value = part[i, rows, cols].astype(F32) + got[i, q, :, cols].astype(F32)
                joined[i, q, :, cols] = value.astype(BF16)

            over_columns(add)
            rs_pass(i, 4 + q, joined.at[i, q], to)

    def rs3(i):
        for q, source in ((2, behind), (3, ahead), (4, behind), (5, ahead)):
            rs_wait(i, q, source)
        far_piece, near_piece = 1 - y_lo, y_lo

        def add_far(cols):
            value = part[i, p_rows(2 * x + far_piece), cols].astype(F32)
            value = value + got[i, 4 + far_piece, :, cols].astype(F32) + got[i, 3 - far_piece, :, cols].astype(F32)
            joined[i, 2, :, cols] = value.astype(BF16)

        over_columns(add_far)
        rs_pass(i, 6, joined.at[i, 2], beside)

        def add_near(cols):
            value = part[i, p_rows(2 * x + near_piece), cols].astype(F32)
            value = value + got[i, 4 + near_piece, :, cols].astype(F32) + got[i, 3 - near_piece, :, cols].astype(F32)
            kept[i, :, cols] = value

        over_columns(add_near)

    def move(src, dst, send_sem, recv_sem, to, stays):
        @pl.when(stays)
        def _():
            pltpu.make_async_copy(src, dst, recv_sem).start()

        copy = pltpu.make_async_remote_copy(
            src_ref=src, dst_ref=dst, send_sem=send_sem, recv_sem=recv_sem, device_id=to, device_id_type=MESH
        )

        @pl.when(jnp.logical_not(stays))
        def _():
            copy.start()

        moves.append((copy, stays))

    def rs4(i):
        rs_wait(i, 6, beside)

        def add(cols):
            summed[i, :, cols] = (kept[i, :, cols] + got[i, 6, :, cols].astype(F32)).astype(BF16)

        over_columns(add)
        move(summed.at[i], passing.at[i], mv_send.at[0, i], mv_recv.at[0, i], z_to, stays_z)

    def rs5(i):
        pltpu.make_async_copy(summed.at[i], passing.at[i], mv_recv.at[0, i]).wait()
        move(passing.at[i], moved.at[i], mv_send.at[1, i], mv_recv.at[1, i], xy_to, stays_xy)

    def merge(i):
        a_copies[i].wait()
        pltpu.make_async_copy(passing.at[i], moved.at[i], mv_recv.at[1, i]).wait()

        @pl.loop(0, width // 256)
        def _(n):
            cols = pl.ds(pl.multiple_of(n * 256, 256), 256)
            dst = pl.ds(pl.multiple_of(core * width + n * 256, 128), 256)
            a_part = a_buf[i, :, :, cols].reshape(PIECE, 256).astype(F32)
            value = 0.5 * (a_part + moved[i, :, cols].astype(F32))
            merged[i, p_rows(mine), dst] = value.astype(BF16)

        ag1(1, m_ref, i)

    out_copies = []

    def write_out(i):
        if i < 2:
            for c in range(16):
                copy = pltpu.make_async_copy(
                    merged.at[i, pl.ds(c * BLOCK, BLOCK), :], out_gate_up.at[c, i], local_sem.at[8 + i * 16 + c]
                )
                copy.start()
                out_copies.append(copy)
        else:
            copy = pltpu.make_async_copy(merged.at[2], out_down, local_sem.at[40])
            copy.start()
            out_copies.append(copy)

    def gate_up(first, last):
        @pl.loop(first, last)
        def _(n):
            cols = pl.ds(pl.multiple_of(n * 256, 256), 256)
            contract = (((0,), (0,)), ((), ()))
            weights = jnp.concatenate([merged[0, 0:128, cols], merged[1, 0:128, cols]], axis=0)
            gate = lax.dot_general(weights, tok_t[...], contract, preferred_element_type=F32) * R ** (-0.5)
            weights = jnp.concatenate([merged[0, 128:256, cols], merged[1, 128:256, cols]], axis=0)
            value = lax.dot_general(weights, tok_t[...], contract, preferred_element_type=F32) * R ** (-0.5)
            hidden[cols, :] = (gate * (0.5 + 0.5 * jnp.tanh(0.5 * gate)) * value).astype(BF16)

    def down_half(h):
        toks = pl.ds(h * HALF, HALF)
        value = jnp.dot(merged[2], hidden[:, toks], preferred_element_type=F32)
        total[h] = value
        sent[h] = value.astype(BF16)
        for q, (dx, dy) in enumerate(OFFSETS):
            s = by_row(dx, dy)
            send(sent.at[h, p_rows(s), :], got_check.at[h, q], ck_send.at[h, q], ck_recv.at[h, q], {"row": s, "col": col})

    def finish(h):
        for q, (dx, dy) in enumerate(OFFSETS):
            source = {"row": by_row(4 - dx, dy), "col": col}
            arrived(got_check.at[h, q], ck_send.at[h, q], ck_recv.at[h, q], source)
        value = total[h, p_rows(row), :]
        for q in range(len(OFFSETS)):
            value = value + got_check[h, q].astype(F32)
        out_check[:, h * HALF:(h + 1) * HALF] = (value * FF ** (-0.5)).astype(BF16)

    ag1(0, b_ref, 0)
    tok_copy.wait()
    turned = tok[...].T
    for c in range(8):
        for i in range(2):
            tok_t[i * 128 + c * 16:i * 128 + c * 16 + 16, :] = turned[c * 32 + i * 16:c * 32 + i * 16 + 16, :]
    ag2(0, b_ref, 0)
    ag1(0, b_ref, 1)
    ag3(0, b_ref, 0)
    t_copy.wait()
    matmul(0, 0, 4)
    ag2(0, b_ref, 1)
    ag1(0, b_ref, 2)
    matmul(0, 4, 7)
    rs1(0)
    ag3(0, b_ref, 1)
    rs2(0)
    matmul(1, 0, 4)
    ag2(0, b_ref, 2)
    matmul(1, 4, 7)
    rs1(1)
    rs3(0)
    ag3(0, b_ref, 2)
    rs2(1)
    rs4(0)
    matmul(2, 0, 4)
    rs5(0)
    matmul(2, 4, 7)
    rs1(2)
    merge(0)
    rs3(1)
    rs4(1)
    rs2(2)
    rs5(1)
    ag2(1, m_ref, 0)
    merge(1)
    rs3(2)
    rs4(2)
    ag3(1, m_ref, 0)
    rs5(2)
    ag2(1, m_ref, 1)
    merge(2)
    write_out(0)
    ag3(1, m_ref, 1)
    write_out(1)
    gate_up(0, 5)
    ag2(1, m_ref, 2)
    gate_up(5, 14)
    ag3(1, m_ref, 2)
    write_out(2)
    down_half(0)
    down_half(1)
    finish(0)
    finish(1)
    for copy in out_copies:
        copy.wait()
    for copy in started:
        copy.wait_send()
    for copy, stays in moves:
        @pl.when(jnp.logical_not(stays))
        def _(copy=copy):
            copy.wait_send()


def on_device(b_gate_up, b_down, a_gate_up, a_down, transform, check_tokens):
    depth, width = transform.shape
    toks = check_tokens.shape[0]
    anywhere = pl.BlockSpec(memory_space=pl.ANY)
    merged_gate_up, merged_down, check = pl.pallas_call(
        kernel,
        out_shape=(
            jax.ShapeDtypeStruct((16, 2, BLOCK, depth), BF16),
            jax.ShapeDtypeStruct((CHUNK, depth), BF16),
            jax.ShapeDtypeStruct((PIECE, toks), BF16),
        ),
        in_specs=[anywhere] * 6,
        out_specs=(anywhere, anywhere, pl.BlockSpec(memory_space=pltpu.VMEM)),
        scratch_shapes=[
            pltpu.VMEM((depth, width), BF16),
            pltpu.VMEM((3, CHUNK, depth), BF16),
            pltpu.VMEM((3, CHUNK, width), BF16),
            pltpu.VMEM((3, 7, PIECE, width), BF16),
            pltpu.VMEM((3, 3, PIECE, width), BF16),
            pltpu.VMEM((3, PIECE, width), F32),
            pltpu.VMEM((3, PIECE, width), BF16),
            pltpu.VMEM((3, PIECE, width), BF16),
            pltpu.VMEM((3, PIECE, width), BF16),
            pltpu.VMEM((3, 2, BLOCK, width), BF16),
            pltpu.VMEM((3, CHUNK, depth), BF16),
            pltpu.VMEM((toks, R), BF16),
            pltpu.VMEM((R, toks), BF16),
            pltpu.VMEM((depth, toks), BF16),
            pltpu.VMEM((2, CHUNK, HALF), F32),
            pltpu.VMEM((2, CHUNK, HALF), BF16),
            pltpu.VMEM((2, 7, PIECE, HALF), BF16),
            pltpu.SemaphoreType.DMA((41,)),
            pltpu.SemaphoreType.DMA((2, 3, 15)),
            pltpu.SemaphoreType.DMA((2, 3, 15)),
            pltpu.SemaphoreType.DMA((3, 7)),
            pltpu.SemaphoreType.DMA((3, 7)),
            pltpu.SemaphoreType.DMA((2, 3)),
            pltpu.SemaphoreType.DMA((2, 3)),
            pltpu.SemaphoreType.DMA((2, 7)),
            pltpu.SemaphoreType.DMA((2, 7)),
        ],
        compiler_params=pltpu.CompilerParams(
            collective_id=0, has_side_effects=True, vmem_limit_bytes=60 * 1024 * 1024
        ),
        name="merge_and_check",
    )(
        b_gate_up,
        b_down,
        a_gate_up.reshape(16, 2, BLOCK, depth),
        a_down.reshape(16, BLOCK, depth),
        transform,
        check_tokens,
    )
    return merged_gate_up.reshape(2 * R, depth), merged_down, check.T


def solution(mesh):
    return jax.shard_map(
        on_device,
        mesh=mesh,
        in_specs=(
            P("col", "row"),
            P("col", "row"),
            P(None, "row"),
            P(None, "row"),
            P("row", "col"),
            P("col", None),
        ),
        out_specs=(P(None, "row"), P(None, "row"), P("col", "row")),
        check_vma=False,
    )
```

```python
import jax
import jax.numpy as jnp
from jax import lax
from jax.experimental import pallas as pl
from jax.experimental.pallas import tpu as pltpu
from jax.sharding import PartitionSpec as P

FF = 28672
R = 256
MESH = pl.DeviceIdType.MESH
BF16 = jnp.bfloat16
F32 = jnp.float32
CHUNK, BLOCK, PIECE = 256, 16, 32
OFFSETS = ((2, 1), (2, 0), (1, 1), (3, 1), (1, 0), (3, 0), (0, 1))
HALF = 512
PARTS = ((0, 1024), (1024, 768))
ORDER = """
A1.0 T A2y.0 A2f.0 A1.1 A3.0 A2n.0 A4.0 A2f.1 A2y.1 M.0a R1.0a
A1.2 M.0b A2n.1 R1.0b A3.1 R2.0a A2y.2 A4.1 A2f.2 R2.0b M.1a R1.1a
A2n.2 R3.0a M.1b R2.1a R4.0a R1.1b A3.2 R3.0b R3.1a A4.2 R4.0b R5.0a
R2.1b M.2a R4.1a R5.0b R1.2a R3.1b D1.0a M.2b R5.1a R2.2a R4.1b D1.0b
R1.2b D2y.0a D2f.0a R5.1b R3.2a D1.1a R2.2b D2n.0b R4.2a R3.2b D1.1b D3.0a
D2f.1a D2n.1a R4.2b D2n.0a R5.2a D2y.1a D2f.1b D4.0a D2f.0b D2y.1b D2n.1b R5.2b
D2y.0b D3.1a D1.2a D3.1b D4.1a Ga0 D1.2b D2y.2a D2f.2a D3.0b Ga1 D4.1b
D2f.2b D2y.2b D2n.2a D4.0b Gb1 D2n.2b D3.2a Gb0 D4.2a D3.2b Ha D4.2b
Hb F0 F1
""".split()


def device(x, y, z, core):
    x, y, z = lax.rem(x + 8, 4), lax.rem(y + 8, 4), lax.rem(z + 8, 4)
    return {"row": lax.rem(y, 2) * 4 + x, "col": z * 4 + (y // 2) * 2 + core}


def kernel(
    b_gate_up, b_down, a_gate_up, a_down, transform, tokens,
    out_gate_up, out_down, out_check,
    t_buf, b_buf, part, got, joined, kept, summed, passing, moved, a_buf, merged, tok, tok_t, hidden, total, sent, got_check,
    local_sem, ag_send, ag_recv, rs_send, rs_recv, mv_send, mv_recv, ck_send, ck_recv,
):
    row, col = lax.axis_index("row"), lax.axis_index("col")
    x, y_lo = lax.rem(row, 4), row // 4
    z, y_hi, core = col // 4, lax.rem(col // 2, 2), lax.rem(col, 2)
    y = y_hi * 2 + y_lo
    other_core = 1 - core
    group = col // 2
    width = t_buf.shape[1]
    started, moves, waited_a = [], [], set()

    def pair(z_off, flip):
        return lax.rem(z + z_off + 4, 4) * 2 + (1 - y_hi if flip else y_hi)

    def b_ref(i, g, k):
        return b_buf.at[i, pl.ds(pl.multiple_of((g * 2 + k) * BLOCK, BLOCK), BLOCK), :]

    from_z, from_y = row // 2, lax.rem(row, 2)

    def piece_of(g):
        return 2 * lax.rem(g // 2 - from_z + x + 6, 4) + lax.rem(g + from_y + y_lo, 2)

    def m_ref(j, g, k):
        first, wide = PARTS[j % 2]
        rows = pl.ds(pl.multiple_of(piece_of(g) * PIECE, PIECE), PIECE)
        return merged.at[j // 2, rows, pl.ds(pl.multiple_of(k * width + first, 128), wide)]

    def cols_of(j):
        return pl.ds(*PARTS[j % 2])

    def p_rows(s):
        return pl.ds(pl.multiple_of(s * PIECE, PIECE), PIECE)

    up, down, far = device(x, y, z + 1, core), device(x, y, z - 1, core), device(x, y, z + 2, core)
    across, partner = device(x, y + 2, z, core), device(x, y, z, other_core)

    def by_row(dx, dy):
        return lax.rem(x + dx, 4) + 4 * lax.rem(y_lo + dy, 2)

    hop_z = lax.rem(z + x - 2 * lax.rem(z, 2) - y_hi + 7 + 3, 4)
    stays_z = hop_z == z
    lag = lax.rem(z - x + y_hi + 4, 4)
    src_z = lax.rem(lag + 2 * (1 - lax.rem(lag, 2)), 4)
    to_x, to_y_lo = 2 * lax.rem(src_z, 2) + y_hi, src_z // 2
    to_y_hi = lax.rem(y_hi + y_lo + to_y_lo, 2)
    stays_xy = (to_x == x) & (to_y_lo == y_lo) & (to_y_hi == y_hi)
    z_to, z_from = device(x, y, hop_z, core), device(x, y, src_z, core)
    xy_to = device(to_x, to_y_hi * 2 + to_y_lo, z, core)
    xy_from = device(z - from_z + x + 2, from_y * 2 + lax.rem(y_hi + from_y + y_lo, 2), z, core)
    ahead, behind, beside = device(x + 1, y, z, core), device(x - 1, y, z, core), device(x, y + 1 - 2 * y_lo, z, core)

    t_copy = pltpu.make_async_copy(transform, t_buf, local_sem.at[0])
    own = []
    for i in range(3):
        src = b_gate_up.at[pl.ds(i * BLOCK, BLOCK), :] if i < 2 else b_down
        own.append(pltpu.make_async_copy(src, b_ref(i, group, core), local_sem.at[1 + i]))
        own[i].start()
    t_copy.start()
    tok_copy = pltpu.make_async_copy(tokens, tok, local_sem.at[4])
    tok_copy.start()
    mine = piece_of(group)
    a_copies = []
    for i in range(3):
        pairs, cols = pl.ds(mine * 2, 2), pl.ds(pl.multiple_of(core * width, 128), width)
        src = a_gate_up.at[pairs, i, :, cols] if i < 2 else a_down.at[pairs, :, cols]
        a_copies.append(pltpu.make_async_copy(src, a_buf.at[i], local_sem.at[5 + i]))
        a_copies[i].start()

    barrier = pltpu.get_barrier_semaphore()
    peers = [up, down, far, across, partner, ahead, behind, beside, z_to, z_from, xy_to, xy_from]
    peers += [{"row": by_row(dx, dy), "col": col} for dx, dy in OFFSETS]
    for peer in peers:
        pl.semaphore_signal(barrier, inc=1, device_id=peer, device_id_type=MESH)
    for i in range(3):
        own[i].wait()
    pl.semaphore_wait(barrier, len(peers))

    def send(src, dst, send_sem, recv_sem, to):
        copy = pltpu.make_async_remote_copy(
            src_ref=src, dst_ref=dst, send_sem=send_sem, recv_sem=recv_sem, device_id=to, device_id_type=MESH
        )
        copy.start()
        started.append(copy)

    def arrived(dst, send_sem, recv_sem, source):
        pltpu.make_async_remote_copy(
            src_ref=dst, dst_ref=dst, send_sem=send_sem, recv_sem=recv_sem, device_id=source, device_id_type=MESH
        ).wait_recv()

    def ag_pass(phase, ref, i, q, g, to):
        block = ref(i, g, core)
        send(block, block, ag_send.at[phase, i, q], ag_recv.at[phase, i, q], to)

    def ag_wait(phase, ref, i, q, g, k, source):
        arrived(ref(i, g, k), ag_send.at[phase, i, q], ag_recv.at[phase, i, q], source)

    def ag1(phase, ref, i):
        g = pair(0, False)
        for q, to in ((2, far), (3, across), (0, up), (1, down), (4, partner)):
            ag_pass(phase, ref, i, q, g, to)

    def ag2y(phase, ref, i):
        g = pair(0, True)
        ag_wait(phase, ref, i, 3, g, core, across)
        ag_pass(phase, ref, i, 5, g, up)
        ag_pass(phase, ref, i, 6, g, down)
        ag_pass(phase, ref, i, 8, g, partner)

    def ag2f(phase, ref, i):
        g = pair(2, False)
        ag_wait(phase, ref, i, 2, g, core, far)
        ag_pass(phase, ref, i, 7, g, across)
        ag_pass(phase, ref, i, 9, g, partner)

    def ag2n(phase, ref, i):
        for q, off, source in ((0, -1, down), (1, 1, up)):
            ag_wait(phase, ref, i, q, pair(off, False), core, source)
            ag_pass(phase, ref, i, 10 + q, pair(off, False), partner)

    def ag3(phase, ref, i):
        for q, off, source in ((5, -1, down), (6, 1, up), (7, 2, across)):
            ag_wait(phase, ref, i, q, pair(off, True), core, source)
            ag_pass(phase, ref, i, q + 7, pair(off, True), partner)

    def ag4(phase, ref, i):
        for q, off, flip in (
            (4, 0, False), (8, 0, True), (9, 2, False), (10, -1, False), (11, 1, False),
            (12, -1, True), (13, 1, True), (14, 2, True),
        ):
            ag_wait(phase, ref, i, q, pair(off, flip), other_core, partner)

    def over_columns(j, body):
        first, wide = PARTS[j % 2]

        @pl.loop(first // 256, (first + wide) // 256)
        def _(n):
            body(pl.ds(pl.multiple_of(n * 256, 256), 256))

    def matmul(j):
        i = j // 2

        def tile(cols):
            part[i, :, cols] = jnp.dot(b_buf[i], t_buf[:, cols], preferred_element_type=F32).astype(BF16)

        over_columns(j, tile)

    def part_piece(j, s):
        return part.at[j // 2, p_rows(lax.rem(s + 8, 8)), cols_of(j)]

    def rs_pass(j, q, src, to):
        send(src, got.at[j // 2, q, :, cols_of(j)], rs_send.at[j, q], rs_recv.at[j, q], to)

    def rs_wait(j, q, source):
        arrived(got.at[j // 2, q, :, cols_of(j)], rs_send.at[j, q], rs_recv.at[j, q], source)

    def rs1(j):
        rs_pass(j, 0, part_piece(j, 2 * x + 4), ahead)
        rs_pass(j, 1, part_piece(j, 2 * x + 5), behind)
        rs_pass(j, 2, part_piece(j, 2 * x + 3), ahead)
        rs_pass(j, 3, part_piece(j, 2 * x - 2), behind)

    def rs2(j):
        i = j // 2
        for q, s, to, source in ((0, 2 * x + 2, ahead, behind), (1, 2 * x - 1, behind, ahead)):
            rs_wait(j, q, source)
            rows = p_rows(lax.rem(s + 8, 8))

            def add(cols, q=q, rows=rows):
                value = part[i, rows, cols].astype(F32) + got[i, q, :, cols].astype(F32)
                joined[i, q, :, cols] = value.astype(BF16)

            over_columns(j, add)
            rs_pass(j, 4 + q, joined.at[i, q, :, cols_of(j)], to)

    def rs3(j):
        i = j // 2
        for q, source in ((2, behind), (3, ahead), (4, behind), (5, ahead)):
            rs_wait(j, q, source)

        def summed_piece(h, cols):
            value = part[i, p_rows(2 * x + h), cols].astype(F32)
            return value + got[i, 4 + h, :, cols].astype(F32) + got[i, 3 - h, :, cols].astype(F32)

        def add_far(cols):
            joined[i, 2, :, cols] = summed_piece(1 - y_lo, cols).astype(BF16)

        over_columns(j, add_far)
        rs_pass(j, 6, joined.at[i, 2, :, cols_of(j)], beside)

        def add_near(cols):
            kept[i, :, cols] = summed_piece(y_lo, cols)

        over_columns(j, add_near)

    def move(leg, j, src, dst, to, stays):
        src, dst = src.at[j // 2, :, cols_of(j)], dst.at[j // 2, :, cols_of(j)]

        @pl.when(stays)
        def _():
            pltpu.make_async_copy(src, dst, mv_recv.at[leg, j]).start()

        copy = pltpu.make_async_remote_copy(
            src_ref=src, dst_ref=dst, send_sem=mv_send.at[leg, j], recv_sem=mv_recv.at[leg, j],
            device_id=to, device_id_type=MESH,
        )

        @pl.when(jnp.logical_not(stays))
        def _():
            copy.start()

        moves.append((copy, stays))

    def moved_in(leg, j, dst):
        dst = dst.at[j // 2, :, cols_of(j)]
        pltpu.make_async_copy(dst, dst, mv_recv.at[leg, j]).wait()

    def rs4(j):
        i = j // 2
        rs_wait(j, 6, beside)

        def add(cols):
            summed[i, :, cols] = (kept[i, :, cols] + got[i, 6, :, cols].astype(F32)).astype(BF16)

        over_columns(j, add)
        move(0, j, summed, passing, z_to, stays_z)

    def rs5(j):
        moved_in(0, j, passing)
        move(1, j, passing, moved, xy_to, stays_xy)

    def merge(j):
        i = j // 2
        if j not in waited_a:
            a_copies[i].wait()
            waited_a.update((2 * i, 2 * i + 1))
        moved_in(1, j, moved)

        def tile(cols):
            a_part = a_buf[i, :, :, cols].reshape(PIECE, 256).astype(F32)
            value = 0.5 * (a_part + moved[i, :, cols].astype(F32))
            dst = pl.ds(pl.multiple_of(core * width + cols.start, 128), 256)
            merged[i, p_rows(mine), dst] = value.astype(BF16)

        over_columns(j, tile)
        ag1(1, m_ref, j)

    out_copies = []

    def write_out(i):
        if i < 2:
            for c in range(16):
                copy = pltpu.make_async_copy(
                    merged.at[i, pl.ds(c * BLOCK, BLOCK), :], out_gate_up.at[c, i], local_sem.at[8 + i * 16 + c]
                )
                copy.start()
                out_copies.append(copy)
        else:
            copy = pltpu.make_async_copy(merged.at[2], out_down, local_sem.at[40])
            copy.start()
            out_copies.append(copy)

    def gate_up(h, k):
        first, wide = PARTS[h]

        @pl.loop(0, wide // 256)
        def _(n):
            cols = pl.ds(pl.multiple_of(k * width + first + n * 256, 256), 256)
            contract = (((0,), (0,)), ((), ()))
            weights = jnp.concatenate([merged[0, 0:128, cols], merged[1, 0:128, cols]], axis=0)
            gate = lax.dot_general(weights, tok_t[...], contract, preferred_element_type=F32) * R ** (-0.5)
            weights = jnp.concatenate([merged[0, 128:256, cols], merged[1, 128:256, cols]], axis=0)
            value = lax.dot_general(weights, tok_t[...], contract, preferred_element_type=F32) * R ** (-0.5)
            hidden[cols, :] = (gate * (0.5 + 0.5 * jnp.tanh(0.5 * gate)) * value).astype(BF16)

    def down_part(h, begin, end):
        first, wide = PARTS[h]
        for t in range(2):
            toks = pl.ds(t * HALF, HALF)
            value = None if begin else total[t]
            for k in range(2):
                cols = pl.ds(k * width + first, wide)
                more = jnp.dot(merged[2, :, cols], hidden[cols, toks], preferred_element_type=F32)
                value = more if value is None else value + more
            total[t] = value
            if end:
                send_check(t, value)

    def send_check(h, value):
        sent[h] = value.astype(BF16)
        for q, (dx, dy) in enumerate(OFFSETS):
            s = by_row(dx, dy)
            send(sent.at[h, p_rows(s), :], got_check.at[h, q], ck_send.at[h, q], ck_recv.at[h, q], {"row": s, "col": col})

    def finish(h):
        for q, (dx, dy) in enumerate(OFFSETS):
            source = {"row": by_row(4 - dx, dy), "col": col}
            arrived(got_check.at[h, q], ck_send.at[h, q], ck_recv.at[h, q], source)
        value = total[h, p_rows(row), :]
        for q in range(len(OFFSETS)):
            value = value + got_check[h, q].astype(F32)
        out_check[:, h * HALF:(h + 1) * HALF] = (value * FF ** (-0.5)).astype(BF16)

    def turn():
        tok_copy.wait()
        turned = tok[...].T
        for c in range(8):
            for i in range(2):
                tok_t[i * 128 + c * 16:i * 128 + c * 16 + 16, :] = turned[c * 32 + i * 16:c * 32 + i * 16 + 16, :]

    def drain():
        for copy in started:
            copy.wait_send()
        started.clear()
        for copy, stays in moves:
            @pl.when(jnp.logical_not(stays))
            def _(copy=copy):
                copy.wait_send()
        moves.clear()

    gathers = {"1": ag1, "2y": ag2y, "2f": ag2f, "2n": ag2n, "3": ag3, "4": ag4}
    reduces = {"R1": rs1, "R2": rs2, "R3": rs3, "R4": rs4, "R5": rs5, "M": matmul, "D1": merge}
    seen, downs = [], [step for step in ORDER if step[0] == "H"]

    def run(step):
        name, _, where = step.partition(".")
        j = 2 * int(where[0]) + "ab".index(where[1]) if len(where) == 2 else -1
        if step == "T":
            turn()
        elif name[0] == "A":
            gathers[name[1:]](0, b_ref, int(where))
        elif name in reduces:
            if step[0] == "M" and "M" not in seen:
                t_copy.wait()
            reduces[name](j)
        elif name[0] == "D":
            gathers[name[1:]](1, m_ref, j)
            if name == "D4":
                seen.append(where[0])
                if seen.count(where[0]) == 2:
                    write_out(int(where[0]))
        elif name[0] == "G":
            gate_up("ab".index(name[1]), int(name[2]))
        elif name[0] == "H":
            if step == downs[-1]:
                drain()
            down_part("ab".index(name[1]), step == downs[0], step == downs[-1])
        elif name[0] == "F":
            finish(int(name[1]))
        seen.append(name)

    for step in ORDER:
        run(step)
    for copy in out_copies:
        copy.wait()
    drain()


def on_device(b_gate_up, b_down, a_gate_up, a_down, transform, check_tokens):
    depth, width = transform.shape
    toks = check_tokens.shape[0]
    anywhere = pl.BlockSpec(memory_space=pl.ANY)
    merged_gate_up, merged_down, check = pl.pallas_call(
        kernel,
        out_shape=(
            jax.ShapeDtypeStruct((16, 2, BLOCK, depth), BF16),
            jax.ShapeDtypeStruct((CHUNK, depth), BF16),
            jax.ShapeDtypeStruct((PIECE, toks), BF16),
        ),
        in_specs=[anywhere] * 6,
        out_specs=(anywhere, anywhere, pl.BlockSpec(memory_space=pltpu.VMEM)),
        scratch_shapes=[
            pltpu.VMEM((depth, width), BF16),
            pltpu.VMEM((3, CHUNK, depth), BF16),
            pltpu.VMEM((3, CHUNK, width), BF16),
            pltpu.VMEM((3, 7, PIECE, width), BF16),
            pltpu.VMEM((3, 3, PIECE, width), BF16),
            pltpu.VMEM((3, PIECE, width), F32),
            pltpu.VMEM((3, PIECE, width), BF16),
            pltpu.VMEM((3, PIECE, width), BF16),
            pltpu.VMEM((3, PIECE, width), BF16),
            pltpu.VMEM((3, 2, BLOCK, width), BF16),
            pltpu.VMEM((3, CHUNK, depth), BF16),
            pltpu.VMEM((toks, R), BF16),
            pltpu.VMEM((R, toks), BF16),
            pltpu.VMEM((depth, toks), BF16),
            pltpu.VMEM((2, CHUNK, HALF), F32),
            pltpu.VMEM((2, CHUNK, HALF), BF16),
            pltpu.VMEM((2, 7, PIECE, HALF), BF16),
            pltpu.SemaphoreType.DMA((41,)),
            pltpu.SemaphoreType.DMA((2, 6, 15)),
            pltpu.SemaphoreType.DMA((2, 6, 15)),
            pltpu.SemaphoreType.DMA((6, 7)),
            pltpu.SemaphoreType.DMA((6, 7)),
            pltpu.SemaphoreType.DMA((2, 6)),
            pltpu.SemaphoreType.DMA((2, 6)),
            pltpu.SemaphoreType.DMA((2, 7)),
            pltpu.SemaphoreType.DMA((2, 7)),
        ],
        compiler_params=pltpu.CompilerParams(
            collective_id=0, has_side_effects=True, vmem_limit_bytes=60 * 1024 * 1024
        ),
        name="merge_and_check",
    )(
        b_gate_up,
        b_down,
        a_gate_up.reshape(16, 2, BLOCK, depth),
        a_down.reshape(16, BLOCK, depth),
        transform,
        check_tokens,
    )
    return merged_gate_up.reshape(2 * R, depth), merged_down, check.T


def solution(mesh):
    return jax.shard_map(
        on_device,
        mesh=mesh,
        in_specs=(
            P("col", "row"),
            P("col", "row"),
            P(None, "row"),
            P(None, "row"),
            P("row", "col"),
            P("col", None),
        ),
        out_specs=(P(None, "row"), P(None, "row"), P("col", "row")),
        check_vma=False,
    )
```

```python
import jax
import jax.numpy as jnp
from jax import lax
from jax.experimental import pallas as pl
from jax.experimental.pallas import tpu as pltpu
from jax.sharding import PartitionSpec as P

FF = 28672
R = 256
MESH = pl.DeviceIdType.MESH
BF16 = jnp.bfloat16
F32 = jnp.float32
CHUNK, BLOCK, PIECE = 256, 16, 32
OFFSETS = ((2, 1), (2, 0), (1, 1), (3, 1), (1, 0), (3, 0), (0, 1))
HALF = 512
PARTS = ((0, 1024), (1024, 768))
ORDER = (
    "A1.0", "T", "A2y.0", "A2f.0", "A1.1", "A3.0", "A2n.0", "A4.0", "A2f.1", "A2y.1", "M.0a", "R1.0a",
    "A1.2", "M.0b", "A2n.1", "R1.0b", "A3.1", "R2.0a", "A2y.2", "A4.1", "A2f.2", "R2.0b", "M.1a", "R1.1a",
    "A2n.2", "R3.0a", "M.1b", "R2.1a", "R4.0a", "R1.1b", "A3.2", "R3.0b", "R3.1a", "A4.2", "R4.0b", "R5.0a",
    "R2.1b", "M.2a", "R4.1a", "R5.0b", "R1.2a", "R3.1b", "D1.0a", "M.2b", "R5.1a", "R2.2a", "R4.1b", "D1.0b",
    "R1.2b", "D2y.0a", "D2f.0a", "R5.1b", "R3.2a", "D1.1a", "R2.2b", "D2n.0b", "R4.2a", "R3.2b", "D1.1b", "D3.0a",
    "D2f.1a", "D2n.1a", "R4.2b", "D2n.0a", "R5.2a", "D2y.1a", "D2f.1b", "D4.0a", "D2f.0b", "D2y.1b", "D2n.1b", "R5.2b",
    "D2y.0b", "D3.1a", "D1.2a", "D3.1b", "D4.1a", "Ga0", "D1.2b", "D2y.2a", "D2f.2a", "D3.0b", "Ga1", "D4.1b",
    "D2f.2b", "D2y.2b", "D2n.2a", "D4.0b", "Gb1", "D2n.2b", "D3.2a", "Gb0", "D4.2a", "D3.2b", "Ha", "D4.2b",
    "Hb", "F0", "F1",
)


def device(x, y, z, core):
    x, y, z = lax.rem(x + 8, 4), lax.rem(y + 8, 4), lax.rem(z + 8, 4)
    return {"row": lax.rem(y, 2) * 4 + x, "col": z * 4 + (y // 2) * 2 + core}


def kernel(
    b_gate_up, b_down, a_gate_up, a_down, transform, tokens,
    merged, out_check,
    t_buf, b_buf, part, got, joined, kept, summed, passing, moved, a_buf, tok, tok_t, hidden, total, sent, got_check,
    local_sem, ag_send, ag_recv, rs_send, rs_recv, mv_send, mv_recv, ck_send, ck_recv,
):
    row, col = lax.axis_index("row"), lax.axis_index("col")
    x, y_lo = lax.rem(row, 4), row // 4
    z, y_hi, core = col // 4, lax.rem(col // 2, 2), lax.rem(col, 2)
    y = y_hi * 2 + y_lo
    other_core = 1 - core
    group = col // 2
    width = t_buf.shape[1]
    waited_a = set()

    def pair(z_off, flip):
        return lax.rem(z + z_off + 4, 4) * 2 + (1 - y_hi if flip else y_hi)

    def b_ref(i, g, k):
        return b_buf.at[i, pl.ds(pl.multiple_of((g * 2 + k) * BLOCK, BLOCK), BLOCK), :]

    from_z, from_y = row // 2, lax.rem(row, 2)

    def piece_of(g):
        return 2 * lax.rem(g // 2 - from_z + x + 6, 4) + lax.rem(g + from_y + y_lo, 2)

    def m_ref(j, g, k):
        first, wide = PARTS[j % 2]
        rows = pl.ds(pl.multiple_of(piece_of(g) * PIECE, PIECE), PIECE)
        return merged.at[j // 2, rows, pl.ds(pl.multiple_of(k * width + first, 128), wide)]

    def cols_of(j):
        return pl.ds(*PARTS[j % 2])

    def p_rows(s):
        return pl.ds(pl.multiple_of(s * PIECE, PIECE), PIECE)

    up, down, far = device(x, y, z + 1, core), device(x, y, z - 1, core), device(x, y, z + 2, core)
    across, partner = device(x, y + 2, z, core), device(x, y, z, other_core)

    def by_row(dx, dy):
        return lax.rem(x + dx, 4) + 4 * lax.rem(y_lo + dy, 2)

    hop_z = lax.rem(z + x - 2 * lax.rem(z, 2) - y_hi + 7 + 3, 4)
    stays_z = hop_z == z
    lag = lax.rem(z - x + y_hi + 4, 4)
    src_z = lax.rem(lag + 2 * (1 - lax.rem(lag, 2)), 4)
    to_x, to_y_lo = 2 * lax.rem(src_z, 2) + y_hi, src_z // 2
    to_y_hi = lax.rem(y_hi + y_lo + to_y_lo, 2)
    stays_xy = (to_x == x) & (to_y_lo == y_lo) & (to_y_hi == y_hi)
    z_to, z_from = device(x, y, hop_z, core), device(x, y, src_z, core)
    xy_to = device(to_x, to_y_hi * 2 + to_y_lo, z, core)
    xy_from = device(z - from_z + x + 2, from_y * 2 + lax.rem(y_hi + from_y + y_lo, 2), z, core)
    ahead, behind, beside = device(x + 1, y, z, core), device(x - 1, y, z, core), device(x, y + 1 - 2 * y_lo, z, core)

    t_copy = pltpu.make_async_copy(transform, t_buf, local_sem.at[0])
    own = []
    for i in range(3):
        src = b_gate_up.at[pl.ds(i * BLOCK, BLOCK), :] if i < 2 else b_down
        own.append(pltpu.make_async_copy(src, b_ref(i, group, core), local_sem.at[1 + i]))
        own[i].start()
    t_copy.start()
    tok_copy = pltpu.make_async_copy(tokens, tok, local_sem.at[4])
    tok_copy.start()
    mine = piece_of(group)
    a_copies = []
    for i in range(3):
        pairs, cols = pl.ds(mine * 2, 2), pl.ds(pl.multiple_of(core * width, 128), width)
        src = a_gate_up.at[pairs, i, :, cols] if i < 2 else a_down.at[pairs, :, cols]
        a_copies.append(pltpu.make_async_copy(src, a_buf.at[i], local_sem.at[5 + i]))
        a_copies[i].start()

    barrier = pltpu.get_barrier_semaphore()
    peers = [up, down, far, across, partner, ahead, behind, beside, z_to, z_from, xy_to, xy_from]
    peers += [{"row": by_row(dx, dy), "col": col} for dx, dy in OFFSETS]
    for peer in peers:
        pl.semaphore_signal(barrier, inc=1, device_id=peer, device_id_type=MESH)
    for i in range(3):
        own[i].wait()
    pl.semaphore_wait(barrier, len(peers))

    def send(src, dst, send_sem, recv_sem, to):
        pltpu.make_async_remote_copy(
            src_ref=src, dst_ref=dst, send_sem=send_sem, recv_sem=recv_sem, device_id=to, device_id_type=MESH
        ).start()

    def wait(ref, sem):
        pltpu.make_async_copy(ref, ref, sem).wait()

    def blocks(phase, i, n):
        if phase == 0:
            return b_buf.at[i, pl.ds(0, n * BLOCK), :]
        first, wide = PARTS[i % 2]
        if n * PIECE <= CHUNK:
            return merged.at[i // 2, pl.ds(0, n * PIECE), pl.ds(first, wide)]
        return merged.at[i // 2, pl.ds(0, n * PIECE // 2), pl.ds(0, 2 * wide)]

    def pieces(j, n):
        return part.at[j // 2, pl.ds(0, n * PIECE), cols_of(j)]

    def ag_pass(phase, ref, i, q, g, to):
        block = ref(i, g, core)
        send(block, block, ag_send.at[phase, i], ag_recv.at[phase, i, q], to)

    def ag_wait(phase, i, q, n):
        wait(blocks(phase, i, n), ag_recv.at[phase, i, q])

    def ag1(phase, ref, i):
        g = pair(0, False)
        for q, to in ((0, far), (1, across), (2, up), (2, down), (4, partner)):
            ag_pass(phase, ref, i, q, g, to)

    def ag2y(phase, ref, i):
        g = pair(0, True)
        ag_wait(phase, i, 1, 1)
        for q, to in ((3, up), (3, down), (4, partner)):
            ag_pass(phase, ref, i, q, g, to)

    def ag2f(phase, ref, i):
        g = pair(2, False)
        ag_wait(phase, i, 0, 1)
        ag_pass(phase, ref, i, 3, g, across)
        ag_pass(phase, ref, i, 4, g, partner)

    def ag2n(phase, ref, i):
        ag_wait(phase, i, 2, 2)
        for off in (-1, 1):
            ag_pass(phase, ref, i, 4, pair(off, False), partner)

    def ag3(phase, ref, i):
        ag_wait(phase, i, 3, 3)
        for off in (-1, 1, 2):
            ag_pass(phase, ref, i, 4, pair(off, True), partner)

    def ag4(phase, ref, i):
        ag_wait(phase, i, 4, 8)

    def over_columns(j, body):
        first, wide = PARTS[j % 2]

        @pl.loop(first // 256, (first + wide) // 256)
        def _(n):
            body(pl.ds(pl.multiple_of(n * 256, 256), 256))

    def matmul(j):
        i = j // 2

        def tile(cols):
            part[i, :, cols] = jnp.dot(b_buf[i], t_buf[:, cols], preferred_element_type=F32).astype(BF16)

        over_columns(j, tile)

    def part_piece(j, s):
        return part.at[j // 2, p_rows(lax.rem(s + 8, 8)), cols_of(j)]

    def rs_pass(j, q, src, to):
        kind = 0 if q < 2 else 1 if q < 6 else 2
        send(src, got.at[j // 2, q, :, cols_of(j)], rs_send.at[j], rs_recv.at[j, kind], to)

    def rs1(j):
        rs_pass(j, 0, part_piece(j, 2 * x + 4), ahead)
        rs_pass(j, 1, part_piece(j, 2 * x + 5), behind)
        rs_pass(j, 2, part_piece(j, 2 * x + 3), ahead)
        rs_pass(j, 3, part_piece(j, 2 * x - 2), behind)

    def rs2(j):
        i = j // 2
        wait(pieces(j, 2), rs_recv.at[j, 0])
        for q, s, to in ((0, 2 * x + 2, ahead), (1, 2 * x - 1, behind)):
            rows = p_rows(lax.rem(s + 8, 8))

            def add(cols, q=q, rows=rows):
                value = part[i, rows, cols].astype(F32) + got[i, q, :, cols].astype(F32)
                joined[i, q, :, cols] = value.astype(BF16)

            over_columns(j, add)
            rs_pass(j, 4 + q, joined.at[i, q, :, cols_of(j)], to)

    def rs3(j):
        i = j // 2
        wait(pieces(j, 4), rs_recv.at[j, 1])

        def summed_piece(h, cols):
            value = part[i, p_rows(2 * x + h), cols].astype(F32)
            return value + got[i, 4 + h, :, cols].astype(F32) + got[i, 3 - h, :, cols].astype(F32)

        def add_far(cols):
            joined[i, 2, :, cols] = summed_piece(1 - y_lo, cols).astype(BF16)

        over_columns(j, add_far)
        rs_pass(j, 6, joined.at[i, 2, :, cols_of(j)], beside)

        def add_near(cols):
            kept[i, :, cols] = summed_piece(y_lo, cols)

        over_columns(j, add_near)

    def move(leg, j, src, dst, to, stays):
        src, dst = src.at[j // 2, :, cols_of(j)], dst.at[j // 2, :, cols_of(j)]

        @pl.when(stays)
        def _():
            pltpu.make_async_copy(src, dst, mv_recv.at[leg, j]).start()

        @pl.when(jnp.logical_not(stays))
        def _():
            send(src, dst, mv_send.at[leg], mv_recv.at[leg, j], to)

    def moved_in(leg, j, dst):
        wait(dst.at[j // 2, :, cols_of(j)], mv_recv.at[leg, j])

    def rs4(j):
        i = j // 2
        wait(pieces(j, 1), rs_recv.at[j, 2])

        def add(cols):
            summed[i, :, cols] = (kept[i, :, cols] + got[i, 6, :, cols].astype(F32)).astype(BF16)

        over_columns(j, add)
        move(0, j, summed, passing, z_to, stays_z)

    def rs5(j):
        moved_in(0, j, passing)
        move(1, j, passing, moved, xy_to, stays_xy)

    def merge(j):
        i = j // 2
        if j not in waited_a:
            a_copies[i].wait()
            waited_a.update((2 * i, 2 * i + 1))
        moved_in(1, j, moved)

        def tile(cols):
            a_part = a_buf[i, :, :, cols].reshape(PIECE, 256).astype(F32)
            value = 0.5 * (a_part + moved[i, :, cols].astype(F32))
            dst = pl.ds(pl.multiple_of(core * width + cols.start, 128), 256)
            merged[i, p_rows(mine), dst] = value.astype(BF16)

        over_columns(j, tile)
        ag1(1, m_ref, j)

    def gate_up(h, k):
        first, wide = PARTS[h]

        @pl.loop(0, wide // 256)
        def _(n):
            cols = pl.ds(pl.multiple_of(k * width + first + n * 256, 256), 256)
            contract = (((0,), (0,)), ((), ()))
            weights = jnp.concatenate([merged[0, 0:128, cols], merged[1, 0:128, cols]], axis=0)
            gate = lax.dot_general(weights, tok_t[...], contract, preferred_element_type=F32) * R ** (-0.5)
            weights = jnp.concatenate([merged[0, 128:256, cols], merged[1, 128:256, cols]], axis=0)
            value = lax.dot_general(weights, tok_t[...], contract, preferred_element_type=F32) * R ** (-0.5)
            hidden[cols, :] = (gate * (0.5 + 0.5 * jnp.tanh(0.5 * gate)) * value).astype(BF16)

    def down_part(h, begin, end):
        first, wide = PARTS[h]
        for t in range(2):
            toks = pl.ds(t * HALF, HALF)
            value = None if begin else total[t]
            for k in range(2):
                cols = pl.ds(k * width + first, wide)
                more = jnp.dot(merged[2, :, cols], hidden[cols, toks], preferred_element_type=F32)
                value = more if value is None else value + more
            total[t] = value
            if end:
                send_check(t, value)

    def send_check(h, value):
        sent[h] = value.astype(BF16)
        for q, (dx, dy) in enumerate(OFFSETS):
            s = by_row(dx, dy)
            send(sent.at[h, p_rows(s), :], got_check.at[h, q], ck_send.at[h], ck_recv.at[h], {"row": s, "col": col})

    def finish(h):
        wait(sent.at[h, pl.ds(0, 7 * PIECE), :], ck_recv.at[h])
        value = total[h, p_rows(row), :]
        for q in range(len(OFFSETS)):
            value = value + got_check[h, q].astype(F32)
        out_check[:, h * HALF:(h + 1) * HALF] = (value * FF ** (-0.5)).astype(BF16)

    def turn():
        tok_copy.wait()
        turned = tok[...].T
        for c in range(8):
            for i in range(2):
                tok_t[i * 128 + c * 16:i * 128 + c * 16 + 16, :] = turned[c * 32 + i * 16:c * 32 + i * 16 + 16, :]

    def drain():
        for i in range(3):
            wait(blocks(0, i, 15), ag_send.at[0, i])
        for j in range(6):
            wait(blocks(1, j, 15), ag_send.at[1, j])
            wait(pieces(j, 7), rs_send.at[j])
        for leg, stays in ((0, stays_z), (1, stays_xy)):
            @pl.when(jnp.logical_not(stays))
            def _(leg=leg):
                wait(summed, mv_send.at[leg])

    gathers = {"1": ag1, "2y": ag2y, "2f": ag2f, "2n": ag2n, "3": ag3, "4": ag4}
    reduces = {"R1": rs1, "R2": rs2, "R3": rs3, "R4": rs4, "R5": rs5, "M": matmul, "D1": merge}
    seen, downs = [], [step for step in ORDER if step[0] == "H"]

    def run(step):
        name, _, where = step.partition(".")
        j = 2 * int(where[0]) + "ab".index(where[1]) if len(where) == 2 else -1
        if step == "T":
            turn()
        elif name[0] == "A":
            gathers[name[1:]](0, b_ref, int(where))
        elif name in reduces:
            if step[0] == "M" and "M" not in seen:
                t_copy.wait()
            reduces[name](j)
        elif name[0] == "D":
            gathers[name[1:]](1, m_ref, j)
        elif name[0] == "G":
            gate_up("ab".index(name[1]), int(name[2]))
        elif name[0] == "H":
            if step == downs[-1]:
                drain()
            down_part("ab".index(name[1]), step == downs[0], step == downs[-1])
        elif name[0] == "F":
            finish(int(name[1]))
        seen.append(name)

    for step in ORDER:
        run(step)
    for h in range(2):
        wait(sent.at[h, pl.ds(0, 7 * PIECE), :], ck_send.at[h])


def store_kernel(merged, out_gate_up, out_down, sem):
    pltpu.make_async_copy(merged.at[2], out_down, sem.at[2]).start()
    for c in range(16):
        for i in range(2):
            pltpu.make_async_copy(merged.at[i, pl.ds(c * BLOCK, BLOCK), :], out_gate_up.at[c, i], sem.at[i]).start()
    for i in range(3):
        pltpu.make_async_copy(merged.at[i], merged.at[i], sem.at[i]).wait()


def on_device(b_gate_up, b_down, a_gate_up, a_down, transform, check_tokens):
    depth, width = transform.shape
    toks = check_tokens.shape[0]
    hbm = pl.BlockSpec(memory_space=pltpu.HBM)
    merged, check = pl.pallas_call(
        kernel,
        out_shape=(
            pltpu.VMEM((3, CHUNK, depth), BF16),
            jax.ShapeDtypeStruct((PIECE, toks), BF16),
        ),
        in_specs=[hbm] * 6,
        out_specs=(pl.BlockSpec(memory_space=pltpu.VMEM),) * 2,
        scratch_shapes=[
            pltpu.VMEM((depth, width), BF16),
            pltpu.VMEM((3, CHUNK, depth), BF16),
            pltpu.VMEM((3, CHUNK, width), BF16),
            pltpu.VMEM((3, 7, PIECE, width), BF16),
            pltpu.VMEM((3, 3, PIECE, width), BF16),
            pltpu.VMEM((3, PIECE, width), F32),
            pltpu.VMEM((3, PIECE, width), BF16),
            pltpu.VMEM((3, PIECE, width), BF16),
            pltpu.VMEM((3, PIECE, width), BF16),
            pltpu.VMEM((3, 2, BLOCK, width), BF16),
            pltpu.VMEM((toks, R), BF16),
            pltpu.VMEM((R, toks), BF16),
            pltpu.VMEM((depth, toks), BF16),
            pltpu.VMEM((2, CHUNK, HALF), F32),
            pltpu.VMEM((2, CHUNK, HALF), BF16),
            pltpu.VMEM((2, 7, PIECE, HALF), BF16),
            pltpu.SemaphoreType.DMA((11,)),
            pltpu.SemaphoreType.DMA((2, 6)),
            pltpu.SemaphoreType.DMA((2, 6, 5)),
            pltpu.SemaphoreType.DMA((6,)),
            pltpu.SemaphoreType.DMA((6, 3)),
            pltpu.SemaphoreType.DMA((2,)),
            pltpu.SemaphoreType.DMA((2, 6)),
            pltpu.SemaphoreType.DMA((2,)),
            pltpu.SemaphoreType.DMA((2,)),
        ],
        compiler_params=pltpu.CompilerParams(
            collective_id=0, has_side_effects=True, vmem_limit_bytes=61_400_000
        ),
        name="merge_and_check",
    )(
        b_gate_up,
        b_down,
        a_gate_up.reshape(16, 2, BLOCK, depth),
        a_down.reshape(16, BLOCK, depth),
        transform,
        check_tokens,
    )
    merged_gate_up, merged_down = pl.pallas_call(
        store_kernel,
        out_shape=(
            jax.ShapeDtypeStruct((16, 2, BLOCK, depth), BF16),
            jax.ShapeDtypeStruct((CHUNK, depth), BF16),
        ),
        in_specs=[pl.BlockSpec(memory_space=pltpu.VMEM)],
        out_specs=(hbm, hbm),
        scratch_shapes=[pltpu.SemaphoreType.DMA((3,))],
        compiler_params=pltpu.CompilerParams(vmem_limit_bytes=1024 * 1024),
        name="store_merged",
    )(merged)
    return merged_gate_up.reshape(2 * R, depth), merged_down, check.T


def solution(mesh):
    return jax.shard_map(
        on_device,
        mesh=mesh,
        in_specs=(
            P("col", "row"),
            P("col", "row"),
            P(None, "row"),
            P(None, "row"),
            P("row", "col"),
            P("col", None),
        ),
        out_specs=(P(None, "row"), P(None, "row"), P("col", "row")),
        check_vma=False,
    )
```

```python
import jax
import jax.numpy as jnp
from jax import lax
from jax.experimental import pallas as pl
from jax.experimental.pallas import tpu as pltpu
from jax.sharding import PartitionSpec as P

FF = 28672
R = 256
MESH = pl.DeviceIdType.MESH
BF16 = jnp.bfloat16
F32 = jnp.float32
CHUNK, BLOCK, PIECE = 256, 16, 32
OFFSETS = ((2, 1), (2, 0), (1, 1), (3, 1), (1, 0), (3, 0), (0, 1))
HALF = 512
PARTS = ((0, 1024), (1024, 768))
ORDER = (
    "A1.0", "T", "A2f.0", "A2y.0", "A1.1", "A2n.0", "A3.0", "A4.0", "A2f.1", "A2y.1",
    "A1.2", "M.0a02", "M.0a22", "R1.0a", "M.0b02", "M.0b21", "R1.0b", "A2n.1", "A3.1", "R2.0a",
    "A2f.2", "A2y.2", "A4.1", "M.1a02", "R2.0b", "M.1a22", "R1.1a", "R3.0a", "M.1b02", "M.1b21",
    "R3.0b", "R1.1b", "A3.2", "A2n.2", "R2.1a", "R5.0a", "A4.2", "M.2a02", "R2.1b", "M.2a22",
    "R1.2a", "R5.0b", "R3.1a", "M.2b02", "D1.0a", "M.2b21", "R2.2a", "R3.1b", "R1.2b", "D2y.0a",
    "R5.1a", "R3.2a", "D2n.0a", "D1.0b", "R2.2b", "D2f.0a", "R5.1b", "D1.1a", "R3.2b", "R5.2a",
    "D2y.0b", "D3.0a", "D2f.0b", "D2y.1a", "D2n.0b", "D2f.1a", "D1.1b", "R5.2b", "D2n.1a", "D1.2a",
    "D4.0a", "D2f.1b", "D3.1a", "D2y.1b", "D3.0b", "D2n.1b", "D1.2b", "D4.1a", "G.a022", "D2y.2a",
    "D2f.2a", "D4.0b", "D2n.2a", "G.a122", "D3.1b", "G.a102", "D2f.2b", "D2y.2b", "G.a002", "D4.1b",
    "G.b002", "D3.2a", "D2n.2b", "G.b121", "G.b102", "D3.2b", "G.b021", "D4.2a", "H.a", "D4.2b",
    "H.b", "F.0", "F.1",
)


def device(x, y, z, core):
    x, y, z = lax.rem(x + 8, 4), lax.rem(y + 8, 4), lax.rem(z + 8, 4)
    return {"row": lax.rem(y, 2) * 4 + x, "col": z * 4 + (y // 2) * 2 + core}


def kernel(
    b_gate_up, b_down, a_gate_up, a_down, transform, tokens,
    merged, out_check,
    t_buf, b_buf, part, got, joined, kept, summed, passing, moved, a_buf, tok, tok_t, hidden, total, sent, got_check,
    local_sem, ag_send, ag_recv, rs_send, rs_recv, mv_send, mv_recv, ck_send, ck_recv,
):
    row, col = lax.axis_index("row"), lax.axis_index("col")
    x, y_lo = lax.rem(row, 4), row // 4
    z, y_hi, core = col // 4, lax.rem(col // 2, 2), lax.rem(col, 2)
    y = y_hi * 2 + y_lo
    other_core = 1 - core
    group = col // 2
    width = t_buf.shape[1]
    waited_a = set()

    def pair(z_off, flip):
        return lax.rem(z + z_off + 4, 4) * 2 + (1 - y_hi if flip else y_hi)

    def b_ref(i, g, k):
        return b_buf.at[i, pl.ds(pl.multiple_of((g * 2 + k) * BLOCK, BLOCK), BLOCK), :]

    from_z, from_y = row // 2, lax.rem(row, 2)

    def piece_of(g):
        return 2 * lax.rem(g // 2 - from_z + x + 6, 4) + lax.rem(g + from_y + y_lo, 2)

    def m_ref(j, g, k):
        first, wide = PARTS[j % 2]
        rows = pl.ds(pl.multiple_of(piece_of(g) * PIECE, PIECE), PIECE)
        return merged.at[j // 2, rows, pl.ds(pl.multiple_of(k * width + first, 128), wide)]

    def cols_of(j):
        return pl.ds(*PARTS[j % 2])

    def p_rows(s):
        return pl.ds(pl.multiple_of(s * PIECE, PIECE), PIECE)

    up, down, far = device(x, y, z + 1, core), device(x, y, z - 1, core), device(x, y, z + 2, core)
    across, partner = device(x, y + 2, z, core), device(x, y, z, other_core)

    def by_row(dx, dy):
        return lax.rem(x + dx, 4) + 4 * lax.rem(y_lo + dy, 2)

    hop_z = lax.rem(z + x - 2 * lax.rem(z, 2) - y_hi + 7 + 3, 4)
    stays_z = hop_z == z
    lag = lax.rem(z - x + y_hi + 4, 4)
    src_z = lax.rem(lag + 2 * (1 - lax.rem(lag, 2)), 4)
    to_x, to_y_lo = 2 * lax.rem(src_z, 2) + y_hi, src_z // 2
    to_y_hi = lax.rem(y_hi + y_lo + to_y_lo, 2)
    stays_xy = (to_x == x) & (to_y_lo == y_lo) & (to_y_hi == y_hi)
    z_to, z_from = device(x, y, hop_z, core), device(x, y, src_z, core)
    xy_to = device(to_x, to_y_hi * 2 + to_y_lo, z, core)
    xy_from = device(z - from_z + x + 2, from_y * 2 + lax.rem(y_hi + from_y + y_lo, 2), z, core)
    ahead, behind = device(x + 1, y, z, core), device(x - 1, y, z, core)
    y_beside = y + 1 - 2 * y_lo
    beside_to, beside_from = device(x, y_beside, hop_z, core), device(x, y_beside, src_z, core)

    t_copy = pltpu.make_async_copy(transform, t_buf, local_sem.at[0])
    own = []
    for i in range(3):
        src = b_gate_up.at[pl.ds(i * BLOCK, BLOCK), :] if i < 2 else b_down
        own.append(pltpu.make_async_copy(src, b_ref(i, group, core), local_sem.at[1 + i]))
        own[i].start()
    t_copy.start()
    tok_copy = pltpu.make_async_copy(tokens, tok, local_sem.at[4])
    tok_copy.start()
    mine = piece_of(group)
    a_copies = []
    for i in range(3):
        pairs, cols = pl.ds(mine * 2, 2), pl.ds(pl.multiple_of(core * width, 128), width)
        src = a_gate_up.at[pairs, i, :, cols] if i < 2 else a_down.at[pairs, :, cols]
        a_copies.append(pltpu.make_async_copy(src, a_buf.at[i], local_sem.at[5 + i]))
        a_copies[i].start()

    barrier = pltpu.get_barrier_semaphore()
    peers = [up, down, far, across, partner, ahead, behind, beside_to, beside_from, z_to, z_from, xy_to, xy_from]
    peers += [{"row": by_row(dx, dy), "col": col} for dx, dy in OFFSETS]
    for peer in peers:
        pl.semaphore_signal(barrier, inc=1, device_id=peer, device_id_type=MESH)
    for i in range(3):
        own[i].wait()
    pl.semaphore_wait(barrier, len(peers))

    def send(src, dst, send_sem, recv_sem, to):
        pltpu.make_async_remote_copy(
            src_ref=src, dst_ref=dst, send_sem=send_sem, recv_sem=recv_sem, device_id=to, device_id_type=MESH
        ).start()

    def wait(ref, sem):
        pltpu.make_async_copy(ref, ref, sem).wait()

    def blocks(phase, i, n):
        if phase == 0:
            return b_buf.at[i, pl.ds(0, n * BLOCK), :]
        first, wide = PARTS[i % 2]
        if n * PIECE <= CHUNK:
            return merged.at[i // 2, pl.ds(0, n * PIECE), pl.ds(first, wide)]
        return merged.at[i // 2, pl.ds(0, n * PIECE // 2), pl.ds(0, 2 * wide)]

    def pieces(j, n):
        return part.at[j // 2, pl.ds(0, n * PIECE), cols_of(j)]

    def ag_pass(phase, ref, i, q, g, to):
        block = ref(i, g, core)
        send(block, block, ag_send.at[phase, i], ag_recv.at[phase, i, q], to)

    def ag_wait(phase, i, q, n):
        wait(blocks(phase, i, n), ag_recv.at[phase, i, q])

    def ag1(phase, ref, i):
        g = pair(0, False)
        for q, to in ((0, far), (1, across), (2, up), (2, down), (4, partner)):
            ag_pass(phase, ref, i, q, g, to)

    def ag2y(phase, ref, i):
        g = pair(0, True)
        ag_wait(phase, i, 1, 1)
        for q, to in ((3, up), (3, down), (4, partner)):
            ag_pass(phase, ref, i, q, g, to)

    def ag2f(phase, ref, i):
        g = pair(2, False)
        ag_wait(phase, i, 0, 1)
        ag_pass(phase, ref, i, 3, g, across)
        ag_pass(phase, ref, i, 4, g, partner)

    def ag2n(phase, ref, i):
        ag_wait(phase, i, 2, 2)
        for off in (-1, 1):
            ag_pass(phase, ref, i, 4, pair(off, False), partner)

    def ag3(phase, ref, i):
        ag_wait(phase, i, 3, 3)
        for off in (-1, 1, 2):
            ag_pass(phase, ref, i, 4, pair(off, True), partner)

    def ag4(phase, ref, i):
        ag_wait(phase, i, 4, 8)

    def over_columns(j, body):
        first, wide = PARTS[j % 2]

        @pl.loop(first // 256, (first + wide) // 256)
        def _(n):
            body(pl.ds(pl.multiple_of(n * 256, 256), 256))

    def matmul(j, first, count):
        i, first = j // 2, PARTS[j % 2][0] // 256 + first

        @pl.loop(first, first + count)
        def _(n):
            cols = pl.ds(pl.multiple_of(n * 256, 256), 256)
            part[i, :, cols] = jnp.dot(b_buf[i], t_buf[:, cols], preferred_element_type=F32).astype(BF16)

    def part_piece(j, s):
        return part.at[j // 2, p_rows(lax.rem(s + 8, 8)), cols_of(j)]

    def rs_pass(j, q, src, to):
        kind = 0 if q < 2 else 1 if q < 6 else 2
        send(src, got.at[j // 2, q, :, cols_of(j)], rs_send.at[j], rs_recv.at[j, kind], to)

    def rs1(j):
        rs_pass(j, 0, part_piece(j, 2 * x + 4), ahead)
        rs_pass(j, 1, part_piece(j, 2 * x + 5), behind)
        rs_pass(j, 2, part_piece(j, 2 * x + 3), ahead)
        rs_pass(j, 3, part_piece(j, 2 * x - 2), behind)

    def rs2(j):
        i = j // 2
        wait(pieces(j, 2), rs_recv.at[j, 0])
        for q, s, to in ((0, 2 * x + 2, ahead), (1, 2 * x - 1, behind)):
            rows = p_rows(lax.rem(s + 8, 8))

            def add(cols, q=q, rows=rows):
                value = part[i, rows, cols].astype(F32) + got[i, q, :, cols].astype(F32)
                joined[i, q, :, cols] = value.astype(BF16)

            over_columns(j, add)
            rs_pass(j, 4 + q, joined.at[i, q, :, cols_of(j)], to)

    def rs3(j):
        i = j // 2
        wait(pieces(j, 4), rs_recv.at[j, 1])

        def summed_piece(h, cols):
            value = part[i, p_rows(2 * x + h), cols].astype(F32)
            return value + got[i, 4 + h, :, cols].astype(F32) + got[i, 3 - h, :, cols].astype(F32)

        def add_far(cols):
            joined[i, 2, :, cols] = summed_piece(1 - y_lo, cols).astype(BF16)

        over_columns(j, add_far)
        rs_pass(j, 6, joined.at[i, 2, :, cols_of(j)], beside_to)

        def add_near(cols):
            kept[i, :, cols] = summed_piece(y_lo, cols).astype(BF16)

        over_columns(j, add_near)
        move(0, j, kept, passing, z_to, stays_z)

    def move(leg, j, src, dst, to, stays):
        src, dst = src.at[j // 2, :, cols_of(j)], dst.at[j // 2, :, cols_of(j)]

        @pl.when(stays)
        def _():
            pltpu.make_async_copy(src, dst, mv_recv.at[leg, j]).start()

        @pl.when(jnp.logical_not(stays))
        def _():
            send(src, dst, mv_send.at[leg], mv_recv.at[leg, j], to)

    def moved_in(leg, j, dst):
        wait(dst.at[j // 2, :, cols_of(j)], mv_recv.at[leg, j])

    def rs5(j):
        i = j // 2
        moved_in(0, j, passing)
        wait(pieces(j, 1), rs_recv.at[j, 2])

        def add(cols):
            summed[i, :, cols] = (passing[i, :, cols].astype(F32) + got[i, 6, :, cols].astype(F32)).astype(BF16)

        over_columns(j, add)
        move(1, j, summed, moved, xy_to, stays_xy)

    def merge(j):
        i = j // 2
        if j not in waited_a:
            a_copies[i].wait()
            waited_a.update((2 * i, 2 * i + 1))
        moved_in(1, j, moved)

        def tile(cols):
            a_part = a_buf[i, :, :, cols].reshape(PIECE, 256).astype(F32)
            value = 0.5 * (a_part + moved[i, :, cols].astype(F32))
            dst = pl.ds(pl.multiple_of(core * width + cols.start, 128), 256)
            merged[i, p_rows(mine), dst] = value.astype(BF16)

        over_columns(j, tile)
        ag1(1, m_ref, j)

    def gate_up(h, k, first, count):
        start = k * width + PARTS[h][0]

        @pl.loop(first, first + count)
        def _(n):
            cols = pl.ds(pl.multiple_of(start + n * 256, 256), 256)
            contract = (((0,), (0,)), ((), ()))
            weights = jnp.concatenate([merged[0, 0:128, cols], merged[1, 0:128, cols]], axis=0)
            gate = lax.dot_general(weights, tok_t[...], contract, preferred_element_type=F32) * R ** (-0.5)
            weights = jnp.concatenate([merged[0, 128:256, cols], merged[1, 128:256, cols]], axis=0)
            value = lax.dot_general(weights, tok_t[...], contract, preferred_element_type=F32) * R ** (-0.5)
            hidden[cols, :] = (gate * (0.5 + 0.5 * jnp.tanh(0.5 * gate)) * value).astype(BF16)

    def down_part(h, begin, end):
        first, wide = PARTS[h]
        for t in range(2):
            toks = pl.ds(t * HALF, HALF)
            value = None if begin else total[t]
            for k in range(2):
                cols = pl.ds(k * width + first, wide)
                more = jnp.dot(merged[2, :, cols], hidden[cols, toks], preferred_element_type=F32)
                value = more if value is None else value + more
            total[t] = value
            if end:
                send_check(t, value)

    def send_check(h, value):
        sent[h] = value.astype(BF16)
        for q, (dx, dy) in enumerate(OFFSETS):
            s = by_row(dx, dy)
            send(sent.at[h, p_rows(s), :], got_check.at[h, q], ck_send.at[h], ck_recv.at[h], {"row": s, "col": col})

    def finish(h):
        wait(sent.at[h, pl.ds(0, 7 * PIECE), :], ck_recv.at[h])
        value = total[h, p_rows(row), :]
        for q in range(len(OFFSETS)):
            value = value + got_check[h, q].astype(F32)
        out_check[:, h * HALF:(h + 1) * HALF] = (value * FF ** (-0.5)).astype(BF16)

    def turn():
        tok_copy.wait()
        turned = tok[...].T
        for c in range(8):
            for i in range(2):
                tok_t[i * 128 + c * 16:i * 128 + c * 16 + 16, :] = turned[c * 32 + i * 16:c * 32 + i * 16 + 16, :]

    def drain():
        for i in range(3):
            wait(blocks(0, i, 15), ag_send.at[0, i])
        for j in range(6):
            wait(blocks(1, j, 15), ag_send.at[1, j])
            wait(pieces(j, 7), rs_send.at[j])
        for leg, stays in ((0, stays_z), (1, stays_xy)):
            @pl.when(jnp.logical_not(stays))
            def _(leg=leg):
                wait(summed, mv_send.at[leg])

    gathers = {"1": ag1, "2y": ag2y, "2f": ag2f, "2n": ag2n, "3": ag3, "4": ag4}
    reduces = {"R1": rs1, "R2": rs2, "R3": rs3, "R5": rs5, "D1": merge}
    seen, downs = [], [step for step in ORDER if step[0] == "H"]

    def run(step):
        name, _, where = step.partition(".")
        digits = [int(d) if d.isdigit() else "ab".index(d) for d in where]
        if name == "T":
            turn()
        elif name == "M":
            if not seen:
                t_copy.wait()
                seen.append(step)
            matmul(2 * digits[0] + digits[1], *digits[2:])
        elif name == "G":
            gate_up(*digits)
        elif name == "H":
            if step == downs[-1]:
                drain()
            down_part(digits[0], step == downs[0], step == downs[-1])
        elif name == "F":
            finish(digits[0])
        elif name[0] == "A":
            gathers[name[1:]](0, b_ref, digits[0])
        elif name in reduces:
            reduces[name](2 * digits[0] + digits[1])
        else:
            gathers[name[1:]](1, m_ref, 2 * digits[0] + digits[1])

    for step in ORDER:
        run(step)
    for h in range(2):
        wait(sent.at[h, pl.ds(0, 7 * PIECE), :], ck_send.at[h])


def store_kernel(merged, check, out_gate_up, out_down, out_check, sem):
    check_copy = pltpu.make_async_copy(check, out_check, sem.at[3])
    check_copy.start()
    pltpu.make_async_copy(merged.at[2], out_down, sem.at[2]).start()
    for c in range(16):
        for i in range(2):
            pltpu.make_async_copy(merged.at[i, pl.ds(c * BLOCK, BLOCK), :], out_gate_up.at[c, i], sem.at[i]).start()
    for i in range(3):
        pltpu.make_async_copy(merged.at[i], merged.at[i], sem.at[i]).wait()
    check_copy.wait()


def on_device(b_gate_up, b_down, a_gate_up, a_down, transform, check_tokens):
    depth, width = transform.shape
    toks = check_tokens.shape[0]
    hbm = pl.BlockSpec(memory_space=pltpu.HBM)
    merged, check = pl.pallas_call(
        kernel,
        out_shape=(
            pltpu.VMEM((3, CHUNK, depth), BF16),
            pltpu.VMEM((PIECE, toks), BF16),
        ),
        in_specs=[hbm] * 6,
        out_specs=(pl.BlockSpec(memory_space=pltpu.VMEM),) * 2,
        scratch_shapes=[
            pltpu.VMEM((depth, width), BF16),
            pltpu.VMEM((3, CHUNK, depth), BF16),
            pltpu.VMEM((3, CHUNK, width), BF16),
            pltpu.VMEM((3, 7, PIECE, width), BF16),
            pltpu.VMEM((3, 3, PIECE, width), BF16),
            pltpu.VMEM((3, PIECE, width), BF16),
            pltpu.VMEM((3, PIECE, width), BF16),
            pltpu.VMEM((3, PIECE, width), BF16),
            pltpu.VMEM((3, PIECE, width), BF16),
            pltpu.VMEM((3, 2, BLOCK, width), BF16),
            pltpu.VMEM((toks, R), BF16),
            pltpu.VMEM((R, toks), BF16),
            pltpu.VMEM((depth, toks), BF16),
            pltpu.VMEM((2, CHUNK, HALF), F32),
            pltpu.VMEM((2, CHUNK, HALF), BF16),
            pltpu.VMEM((2, 7, PIECE, HALF), BF16),
            pltpu.SemaphoreType.DMA((11,)),
            pltpu.SemaphoreType.DMA((2, 6)),
            pltpu.SemaphoreType.DMA((2, 6, 5)),
            pltpu.SemaphoreType.DMA((6,)),
            pltpu.SemaphoreType.DMA((6, 3)),
            pltpu.SemaphoreType.DMA((2,)),
            pltpu.SemaphoreType.DMA((2, 6)),
            pltpu.SemaphoreType.DMA((2,)),
            pltpu.SemaphoreType.DMA((2,)),
        ],
        compiler_params=pltpu.CompilerParams(
            collective_id=0, has_side_effects=True, vmem_limit_bytes=61_400_000
        ),
        name="merge_and_check",
    )(
        b_gate_up,
        b_down,
        a_gate_up.reshape(16, 2, BLOCK, depth),
        a_down.reshape(16, BLOCK, depth),
        transform,
        check_tokens,
    )
    merged_gate_up, merged_down, check = pl.pallas_call(
        store_kernel,
        out_shape=(
            jax.ShapeDtypeStruct((16, 2, BLOCK, depth), BF16),
            jax.ShapeDtypeStruct((CHUNK, depth), BF16),
            jax.ShapeDtypeStruct((PIECE, toks), BF16),
        ),
        in_specs=[pl.BlockSpec(memory_space=pltpu.VMEM)] * 2,
        out_specs=(hbm, hbm, hbm),
        scratch_shapes=[pltpu.SemaphoreType.DMA((4,))],
        compiler_params=pltpu.CompilerParams(vmem_limit_bytes=1024 * 1024),
        name="store_merged",
    )(merged, check)
    return merged_gate_up.reshape(2 * R, depth), merged_down, check.T


def solution(mesh):
    return jax.shard_map(
        on_device,
        mesh=mesh,
        in_specs=(
            P("col", "row"),
            P("col", "row"),
            P(None, "row"),
            P(None, "row"),
            P("row", "col"),
            P("col", None),
        ),
        out_specs=(P(None, "row"), P(None, "row"), P("col", "row")),
        check_vma=False,
    )
```

```python
import jax
import jax.numpy as jnp
from jax import lax
from jax.experimental import pallas as pl
from jax.experimental.pallas import tpu as pltpu
from jax.sharding import PartitionSpec as P

FF = 28672
R = 256
MESH = pl.DeviceIdType.MESH
BF16 = jnp.bfloat16
F32 = jnp.float32
CHUNK, BLOCK, PIECE = 256, 16, 32
OFFSETS = ((2, 1), (2, 0), (1, 1), (3, 1), (1, 0), (3, 0), (0, 1))
HALF = 512
PARTS = ((0, 1024), (1024, 768))
ORDER = (
    "A1.0", "T", "A2y.0", "A2f.0", "A1.1", "A2n.0", "A3.0", "A2f.1", "A2y.1", "A1.2",
    "A4.0", "M.0a01", "M.0a11", "M.0a21", "A2n.1", "M.0a31", "R1.0a", "M.0b01", "M.0b11", "M.0b21",
    "R1.0b", "A3.1", "A2f.2", "A2y.2", "R2.0a", "A4.1", "M.1a01", "M.1a11", "R2.0b", "M.1a21",
    "M.1a31", "R1.1a", "A2n.2", "M.1b01", "M.1b11", "R3.0a", "M.1b21", "R3.0b", "R1.1b", "A3.2",
    "R2.1a", "A4.2", "M.2a01", "R2.1b", "M.2a11", "R5.0a", "M.2a21", "M.2a31", "R5.0b", "R3.1a",
    "R1.2a", "R3.1b", "D1.0a", "M.2b01", "R2.2a", "M.2b11", "M.2b21", "R5.1a", "D1.0b", "R1.2b",
    "D2y.0a", "R5.1b", "R3.2a", "D2f.0a", "R2.2b", "D1.1a", "D2n.0b", "D2f.0b", "R3.2b", "R5.2a",
    "D1.1b", "D2n.0a", "D3.0a", "D2f.1a", "D2y.1a", "D2n.1a", "D2y.0b", "R5.2b", "D2y.1b", "D2f.1b",
    "D1.2a", "D3.1a", "D2n.1b", "D4.0a", "D4.1a", "D1.2b", "D3.0b", "G.a022", "G.a122", "D2f.2a",
    "D3.1b", "D2y.2a", "G.a002", "D2y.2b", "D2n.2a", "D2f.2b", "G.a102", "D2n.2b", "D4.0b", "D4.1b",
    "G.b102", "G.b021", "D3.2a", "G.b002", "D3.2b", "G.b121", "D4.2a", "H.a", "D4.2b", "H.b",
    "F.0", "F.1",
)


def device(x, y, z, core):
    x, y, z = lax.rem(x + 8, 4), lax.rem(y + 8, 4), lax.rem(z + 8, 4)
    return {"row": lax.rem(y, 2) * 4 + x, "col": z * 4 + (y // 2) * 2 + core}


def kernel(
    b_gate_up, b_down, a_gate_up, a_down, transform, tokens,
    merged, out_check,
    t_buf, b_buf, part, got, joined, kept, summed, passing, moved, a_buf, tok, tok_t, hidden, total, sent, got_check,
    local_sem, ag_send, ag_recv, rs_send, rs_recv, mv_send, mv_recv, ck_send, ck_recv,
):
    row, col = lax.axis_index("row"), lax.axis_index("col")
    x, y_lo = lax.rem(row, 4), row // 4
    z, y_hi, core = col // 4, lax.rem(col // 2, 2), lax.rem(col, 2)
    y = y_hi * 2 + y_lo
    other_core = 1 - core
    group = col // 2
    width = t_buf.shape[1]
    waited_a = set()

    def pair(z_off, flip):
        return lax.rem(z + z_off + 4, 4) * 2 + (1 - y_hi if flip else y_hi)

    def b_ref(i, g, k):
        return b_buf.at[i, pl.ds(pl.multiple_of((g * 2 + k) * BLOCK, BLOCK), BLOCK), :]

    from_z, from_y = row // 2, lax.rem(row, 2)

    def piece_of(g):
        return 2 * lax.rem(g // 2 - from_z + x + 6, 4) + lax.rem(g + from_y + y_lo, 2)

    def m_ref(j, g, k):
        first, wide = PARTS[j % 2]
        rows = pl.ds(pl.multiple_of(piece_of(g) * PIECE, PIECE), PIECE)
        return merged.at[j // 2, rows, pl.ds(pl.multiple_of(k * width + first, 128), wide)]

    def cols_of(j):
        return pl.ds(*PARTS[j % 2])

    def p_rows(s):
        return pl.ds(pl.multiple_of(s * PIECE, PIECE), PIECE)

    up, down, far = device(x, y, z + 1, core), device(x, y, z - 1, core), device(x, y, z + 2, core)
    across, partner = device(x, y + 2, z, core), device(x, y, z, other_core)

    def by_row(dx, dy):
        return lax.rem(x + dx, 4) + 4 * lax.rem(y_lo + dy, 2)

    hop_z = lax.rem(z + x - 2 * lax.rem(z, 2) - y_hi + 7 + 3, 4)
    stays_z = hop_z == z
    lag = lax.rem(z - x + y_hi + 4, 4)
    src_z = lax.rem(lag + 2 * (1 - lax.rem(lag, 2)), 4)
    to_x, to_y_lo = 2 * lax.rem(src_z, 2) + y_hi, src_z // 2
    to_y_hi = lax.rem(y_hi + y_lo + to_y_lo, 2)
    stays_xy = (to_x == x) & (to_y_lo == y_lo) & (to_y_hi == y_hi)
    z_to, z_from = device(x, y, hop_z, core), device(x, y, src_z, core)
    xy_to = device(to_x, to_y_hi * 2 + to_y_lo, z, core)
    xy_from = device(z - from_z + x + 2, from_y * 2 + lax.rem(y_hi + from_y + y_lo, 2), z, core)
    ahead, behind = device(x + 1, y, z, core), device(x - 1, y, z, core)
    y_beside = y + 1 - 2 * y_lo
    beside_to, beside_from = device(x, y_beside, hop_z, core), device(x, y_beside, src_z, core)

    barrier = pltpu.get_barrier_semaphore()
    peers = [up, down, far, across, partner, ahead, behind, beside_to, beside_from, z_to, z_from, xy_to, xy_from]
    peers += [{"row": by_row(dx, dy), "col": col} for dx, dy in OFFSETS]
    for peer in peers:
        pl.semaphore_signal(barrier, inc=1, device_id=peer, device_id_type=MESH)

    t_copy = pltpu.make_async_copy(transform, t_buf, local_sem.at[0])
    own = []
    for i in range(3):
        src = b_gate_up.at[pl.ds(i * BLOCK, BLOCK), :] if i < 2 else b_down
        own.append(pltpu.make_async_copy(src, b_ref(i, group, core), local_sem.at[1 + i]))
        own[i].start()
    t_copy.start()
    tok_copy = pltpu.make_async_copy(tokens, tok, local_sem.at[4])
    tok_copy.start()
    mine = piece_of(group)
    a_copies = []
    for i in range(3):
        pairs, cols = pl.ds(mine * 2, 2), pl.ds(pl.multiple_of(core * width, 128), width)
        src = a_gate_up.at[pairs, i, :, cols] if i < 2 else a_down.at[pairs, :, cols]
        a_copies.append(pltpu.make_async_copy(src, a_buf.at[i], local_sem.at[5 + i]))
        a_copies[i].start()

    for i in range(3):
        own[i].wait()
    pl.semaphore_wait(barrier, len(peers))

    def send(src, dst, send_sem, recv_sem, to):
        pltpu.make_async_remote_copy(
            src_ref=src, dst_ref=dst, send_sem=send_sem, recv_sem=recv_sem, device_id=to, device_id_type=MESH
        ).start()

    def wait(ref, sem):
        pltpu.make_async_copy(ref, ref, sem).wait()

    def blocks(phase, i, n):
        if phase == 0:
            return b_buf.at[i, pl.ds(0, n * BLOCK), :]
        first, wide = PARTS[i % 2]
        if n * PIECE <= CHUNK:
            return merged.at[i // 2, pl.ds(0, n * PIECE), pl.ds(first, wide)]
        return merged.at[i // 2, pl.ds(0, n * PIECE // 2), pl.ds(0, 2 * wide)]

    def pieces(j, n):
        return part.at[j // 2, pl.ds(0, n * PIECE), cols_of(j)]

    def ag_pass(phase, ref, i, q, g, to):
        block = ref(i, g, core)
        send(block, block, ag_send.at[phase, i], ag_recv.at[phase, i, q], to)

    def ag_wait(phase, i, q, n):
        wait(blocks(phase, i, n), ag_recv.at[phase, i, q])

    def ag1(phase, ref, i):
        g = pair(0, False)
        for q, to in ((0, far), (1, across), (2, up), (2, down), (4, partner)):
            ag_pass(phase, ref, i, q, g, to)

    def ag2y(phase, ref, i):
        g = pair(0, True)
        ag_wait(phase, i, 1, 1)
        for q, to in ((3, up), (3, down), (4, partner)):
            ag_pass(phase, ref, i, q, g, to)

    def ag2f(phase, ref, i):
        g = pair(2, False)
        ag_wait(phase, i, 0, 1)
        ag_pass(phase, ref, i, 3, g, across)
        ag_pass(phase, ref, i, 4, g, partner)

    def ag2n(phase, ref, i):
        ag_wait(phase, i, 2, 2)
        for off in (-1, 1):
            ag_pass(phase, ref, i, 4, pair(off, False), partner)

    def ag3(phase, ref, i):
        ag_wait(phase, i, 3, 3)
        for off in (-1, 1, 2):
            ag_pass(phase, ref, i, 4, pair(off, True), partner)

    def ag4(phase, ref, i):
        ag_wait(phase, i, 4, 8)

    def over_columns(j, body):
        first, wide = PARTS[j % 2]

        @pl.loop(first // 256, (first + wide) // 256)
        def _(n):
            body(pl.ds(pl.multiple_of(n * 256, 256), 256))

    def matmul(j, first, count):
        i, first = j // 2, PARTS[j % 2][0] // 256 + first

        @pl.loop(first, first + count)
        def _(n):
            cols = pl.ds(pl.multiple_of(n * 256, 256), 256)
            part[i, :, cols] = jnp.dot(b_buf[i], t_buf[:, cols], preferred_element_type=F32).astype(BF16)

    def part_piece(j, s):
        return part.at[j // 2, p_rows(lax.rem(s + 8, 8)), cols_of(j)]

    def rs_pass(j, q, src, to):
        kind = 0 if q < 2 else 1 if q < 6 else 2
        send(src, got.at[j // 2, q, :, cols_of(j)], rs_send.at[j], rs_recv.at[j, kind], to)

    def rs1(j):
        rs_pass(j, 0, part_piece(j, 2 * x + 4), ahead)
        rs_pass(j, 1, part_piece(j, 2 * x + 5), behind)
        rs_pass(j, 2, part_piece(j, 2 * x + 3), ahead)
        rs_pass(j, 3, part_piece(j, 2 * x - 2), behind)

    def rs2(j):
        i = j // 2
        wait(pieces(j, 2), rs_recv.at[j, 0])
        for q, s, to in ((0, 2 * x + 2, ahead), (1, 2 * x - 1, behind)):
            rows = p_rows(lax.rem(s + 8, 8))

            def add(cols, q=q, rows=rows):
                value = part[i, rows, cols].astype(F32) + got[i, q, :, cols].astype(F32)
                joined[i, q, :, cols] = value.astype(BF16)

            over_columns(j, add)
            rs_pass(j, 4 + q, joined.at[i, q, :, cols_of(j)], to)

    def rs3(j):
        i = j // 2
        wait(pieces(j, 4), rs_recv.at[j, 1])

        def summed_piece(h, cols):
            value = part[i, p_rows(2 * x + h), cols].astype(F32)
            return value + got[i, 4 + h, :, cols].astype(F32) + got[i, 3 - h, :, cols].astype(F32)

        def add_far(cols):
            joined[i, 2, :, cols] = summed_piece(1 - y_lo, cols).astype(BF16)

        over_columns(j, add_far)
        rs_pass(j, 6, joined.at[i, 2, :, cols_of(j)], beside_to)

        def add_near(cols):
            kept[i, :, cols] = summed_piece(y_lo, cols).astype(BF16)

        over_columns(j, add_near)
        move(0, j, kept, passing, z_to, stays_z)

    def move(leg, j, src, dst, to, stays):
        src, dst = src.at[j // 2, :, cols_of(j)], dst.at[j // 2, :, cols_of(j)]

        @pl.when(stays)
        def _():
            pltpu.make_async_copy(src, dst, mv_recv.at[leg, j]).start()

        @pl.when(jnp.logical_not(stays))
        def _():
            send(src, dst, mv_send.at[leg], mv_recv.at[leg, j], to)

    def moved_in(leg, j, dst):
        wait(dst.at[j // 2, :, cols_of(j)], mv_recv.at[leg, j])

    def rs5(j):
        i = j // 2
        moved_in(0, j, passing)
        wait(pieces(j, 1), rs_recv.at[j, 2])

        def add(cols):
            summed[i, :, cols] = (passing[i, :, cols].astype(F32) + got[i, 6, :, cols].astype(F32)).astype(BF16)

        over_columns(j, add)
        move(1, j, summed, moved, xy_to, stays_xy)

    def merge(j):
        i = j // 2
        if j not in waited_a:
            a_copies[i].wait()
            waited_a.update((2 * i, 2 * i + 1))
        moved_in(1, j, moved)

        def tile(cols):
            a_part = a_buf[i, :, :, cols].reshape(PIECE, 256).astype(F32)
            value = 0.5 * (a_part + moved[i, :, cols].astype(F32))
            dst = pl.ds(pl.multiple_of(core * width + cols.start, 128), 256)
            merged[i, p_rows(mine), dst] = value.astype(BF16)

        over_columns(j, tile)
        ag1(1, m_ref, j)

    def gate_up(h, k, first, count):
        start = k * width + PARTS[h][0]

        @pl.loop(first, first + count)
        def _(n):
            cols = pl.ds(pl.multiple_of(start + n * 256, 256), 256)
            contract = (((0,), (0,)), ((), ()))
            weights = jnp.concatenate([merged[0, 0:128, cols], merged[1, 0:128, cols]], axis=0)
            gate = lax.dot_general(weights, tok_t[...], contract, preferred_element_type=F32) * R ** (-0.5)
            weights = jnp.concatenate([merged[0, 128:256, cols], merged[1, 128:256, cols]], axis=0)
            value = lax.dot_general(weights, tok_t[...], contract, preferred_element_type=F32) * R ** (-0.5)
            hidden[cols, :] = (gate * (0.5 + 0.5 * jnp.tanh(0.5 * gate)) * value).astype(BF16)

    def down_part(h, begin, end):
        first, wide = PARTS[h]
        for t in range(2):
            toks = pl.ds(t * HALF, HALF)
            value = None if begin else total[t]
            for k in range(2):
                cols = pl.ds(k * width + first, wide)
                more = jnp.dot(merged[2, :, cols], hidden[cols, toks], preferred_element_type=F32)
                value = more if value is None else value + more
            total[t] = value
            if end:
                send_check(t, value)

    def send_check(h, value):
        sent[h] = value.astype(BF16)
        for q, (dx, dy) in enumerate(OFFSETS):
            s = by_row(dx, dy)
            send(sent.at[h, p_rows(s), :], got_check.at[h, q], ck_send.at[h], ck_recv.at[h], {"row": s, "col": col})

    def finish(h):
        wait(sent.at[h, pl.ds(0, 7 * PIECE), :], ck_recv.at[h])
        value = total[h, p_rows(row), :]
        for q in range(len(OFFSETS)):
            value = value + got_check[h, q].astype(F32)
        out_check[:, h * HALF:(h + 1) * HALF] = (value * FF ** (-0.5)).astype(BF16)

    def turn():
        tok_copy.wait()
        turned = tok[...].T
        for c in range(8):
            for i in range(2):
                tok_t[i * 128 + c * 16:i * 128 + c * 16 + 16, :] = turned[c * 32 + i * 16:c * 32 + i * 16 + 16, :]

    def drain():
        for i in range(3):
            wait(blocks(0, i, 15), ag_send.at[0, i])
        for j in range(6):
            wait(blocks(1, j, 15), ag_send.at[1, j])
            wait(pieces(j, 7), rs_send.at[j])
        for leg, stays in ((0, stays_z), (1, stays_xy)):
            @pl.when(jnp.logical_not(stays))
            def _(leg=leg):
                wait(summed, mv_send.at[leg])

    gathers = {"1": ag1, "2y": ag2y, "2f": ag2f, "2n": ag2n, "3": ag3, "4": ag4}
    reduces = {"R1": rs1, "R2": rs2, "R3": rs3, "R5": rs5, "D1": merge}
    seen, downs = [], [step for step in ORDER if step[0] == "H"]

    def run(step):
        name, _, where = step.partition(".")
        digits = [int(d) if d.isdigit() else "ab".index(d) for d in where]
        if name == "T":
            turn()
        elif name == "M":
            if not seen:
                t_copy.wait()
                seen.append(step)
            matmul(2 * digits[0] + digits[1], *digits[2:])
        elif name == "G":
            gate_up(*digits)
        elif name == "H":
            down_part(digits[0], step == downs[0], step == downs[-1])
        elif name == "F":
            if digits[0] == 0:
                drain()
            finish(digits[0])
        elif name[0] == "A":
            gathers[name[1:]](0, b_ref, digits[0])
        elif name in reduces:
            reduces[name](2 * digits[0] + digits[1])
        else:
            gathers[name[1:]](1, m_ref, 2 * digits[0] + digits[1])

    for step in ORDER:
        run(step)
    for h in range(2):
        wait(sent.at[h, pl.ds(0, 7 * PIECE), :], ck_send.at[h])


def store_kernel(merged, check, out_gate_up, out_down, out_check, sem):
    check_copy = pltpu.make_async_copy(check, out_check, sem.at[3])
    check_copy.start()
    pltpu.make_async_copy(merged.at[2], out_down, sem.at[2]).start()
    for c in range(16):
        for i in range(2):
            pltpu.make_async_copy(merged.at[i, pl.ds(c * BLOCK, BLOCK), :], out_gate_up.at[c, i], sem.at[i]).start()
    for i in range(3):
        pltpu.make_async_copy(merged.at[i], merged.at[i], sem.at[i]).wait()
    check_copy.wait()


def on_device(b_gate_up, b_down, a_gate_up, a_down, transform, check_tokens):
    depth, width = transform.shape
    toks = check_tokens.shape[0]
    hbm = pl.BlockSpec(memory_space=pltpu.HBM)
    merged, check = pl.pallas_call(
        kernel,
        out_shape=(
            pltpu.VMEM((3, CHUNK, depth), BF16),
            pltpu.VMEM((PIECE, toks), BF16),
        ),
        in_specs=[hbm] * 6,
        out_specs=(pl.BlockSpec(memory_space=pltpu.VMEM),) * 2,
        scratch_shapes=[
            pltpu.VMEM((depth, width), BF16),
            pltpu.VMEM((3, CHUNK, depth), BF16),
            pltpu.VMEM((3, CHUNK, width), BF16),
            pltpu.VMEM((3, 7, PIECE, width), BF16),
            pltpu.VMEM((3, 3, PIECE, width), BF16),
            pltpu.VMEM((3, PIECE, width), BF16),
            pltpu.VMEM((3, PIECE, width), BF16),
            pltpu.VMEM((3, PIECE, width), BF16),
            pltpu.VMEM((3, PIECE, width), BF16),
            pltpu.VMEM((3, 2, BLOCK, width), BF16),
            pltpu.VMEM((toks, R), BF16),
            pltpu.VMEM((R, toks), BF16),
            pltpu.VMEM((depth, toks), BF16),
            pltpu.VMEM((2, CHUNK, HALF), F32),
            pltpu.VMEM((2, CHUNK, HALF), BF16),
            pltpu.VMEM((2, 7, PIECE, HALF), BF16),
            pltpu.SemaphoreType.DMA((11,)),
            pltpu.SemaphoreType.DMA((2, 6)),
            pltpu.SemaphoreType.DMA((2, 6, 5)),
            pltpu.SemaphoreType.DMA((6,)),
            pltpu.SemaphoreType.DMA((6, 3)),
            pltpu.SemaphoreType.DMA((2,)),
            pltpu.SemaphoreType.DMA((2, 6)),
            pltpu.SemaphoreType.DMA((2,)),
            pltpu.SemaphoreType.DMA((2,)),
        ],
        compiler_params=pltpu.CompilerParams(
            collective_id=0, has_side_effects=True, vmem_limit_bytes=61_400_000
        ),
        name="merge_and_check",
    )(
        b_gate_up,
        b_down,
        a_gate_up.reshape(16, 2, BLOCK, depth),
        a_down.reshape(16, BLOCK, depth),
        transform,
        check_tokens,
    )
    merged_gate_up, merged_down, check = pl.pallas_call(
        store_kernel,
        out_shape=(
            jax.ShapeDtypeStruct((16, 2, BLOCK, depth), BF16),
            jax.ShapeDtypeStruct((CHUNK, depth), BF16),
            jax.ShapeDtypeStruct((PIECE, toks), BF16),
        ),
        in_specs=[pl.BlockSpec(memory_space=pltpu.VMEM)] * 2,
        out_specs=(hbm, hbm, hbm),
        scratch_shapes=[pltpu.SemaphoreType.DMA((4,))],
        compiler_params=pltpu.CompilerParams(vmem_limit_bytes=1024 * 1024),
        name="store_merged",
    )(merged, check)
    return merged_gate_up.reshape(2 * R, depth), merged_down, check.T


def solution(mesh):
    return jax.shard_map(
        on_device,
        mesh=mesh,
        in_specs=(
            P("col", "row"),
            P("col", "row"),
            P(None, "row"),
            P(None, "row"),
            P("row", "col"),
            P("col", None),
        ),
        out_specs=(P(None, "row"), P(None, "row"), P("col", "row")),
        check_vma=False,
    )
```
